32 devices in a mesh: term: 2 (over x), sector: 16 (over z, y, core).
Axes of the slice: x: 2, y: 2, z: 4, core: 2. Of those that a mesh axis runs over, the one named last changes fastest.
Arguments:
- psi_start: bfloat16 [128, 256, 256], P('sector'), may hold values from -6 to 6
- left_env: bfloat16 [6, 128, 256, 256], P('term', 'sector')
- right_env: bfloat16 [6, 128, 256, 256], P('term', 'sector')
- connect: int32 [6, 128], P('term', 'sector'), may hold values from 0 to 127, as said below
- sector_dims: int32 [2, 128], P(None, 'sector'), may hold values from 64 to 256
- precond: bfloat16 [128, 256, 256], P('sector'), may hold values from 0.5 to 4
Outputs:
- projected: float32 [3, 3], replicated
- last_vector: float32 [128, 256, 256], P('sector', 'term')
- new_env: bfloat16 [6, 128, 256, 256], P('term', 'sector')
The draws below stay inside these ranges and needn't reach their ends.
Inputs may be any that keep to these rules, and one draw needn't show every extreme that they name: connect[t, s] differs from s by at most 8.
All inputs are finite; a program needn't handle non-finite values.
Results may differ from the reference program's by a relative error of at most 0.012.
Values may be sent and summed in bfloat16 or wider, within the bound.
A program may use at most 128 MiB of HBM per device.

```python
import math
import jax
import jax.numpy as jnp
from jax import lax

DB = 256
SD = 8
TD = 3
SECTORS = 128
TERMS = 6


identity_weight = 0.06


drawn_spread = 0.5


shifted_spread = 0.3


def shift_terms():
    return jnp.arange(TERMS) % TD == TD - 1


def unit_diagonal():
    row_ids = lax.broadcasted_iota(jnp.int32, (DB, DB), 0)
    col_ids = lax.broadcasted_iota(jnp.int32, (DB, DB), 1)
    return (row_ids == col_ids).astype(jnp.float32)


def draw_left_env(key, part):
    noise_key, device_key, sector_key = jax.random.split(jax.random.fold_in(key, 17), 3)
    full_shape = (TERMS, SECTORS, DB, DB)
    noise = jax.random.normal(noise_key, full_shape, jnp.float32)
    scaled = noise * DB ** (-0.5)
    device_scale = jnp.exp(jax.random.uniform(device_key, (SECTORS // SD,), jnp.float32, math.log(0.1), math.log(1.0)))
    sector_scale = jnp.exp(jax.random.uniform(sector_key, (SECTORS,), jnp.float32, math.log(0.6), math.log(1.6)))
    energies = jnp.repeat(device_scale, SD) * sector_scale
    shifted = identity_weight * (energies[None, :, None, None] * unit_diagonal()[None, None] + shifted_spread * scaled)
    drawn = drawn_spread * scaled
    return jnp.where(shift_terms()[:, None, None, None], shifted, drawn).astype(jnp.bfloat16)


def draw_right_env(key, part):
    noise_key = jax.random.fold_in(key, 29)
    full_shape = (TERMS, SECTORS, DB, DB)
    noise = jax.random.normal(noise_key, full_shape, jnp.float32)
    scaled = noise * DB ** (-0.5)
    shift_count = TERMS // TD
    right_scale = 2.0 / (shift_count * identity_weight)
    shifted = right_scale * (unit_diagonal()[None, None] + shifted_spread * scaled)
    drawn = drawn_spread * scaled
    return jnp.where(shift_terms()[:, None, None, None], shifted, drawn).astype(jnp.bfloat16)


def draw_connect(key, part):
    offsets = jax.random.randint(jax.random.fold_in(key, 5), (TERMS, SECTORS), -SD, SD + 1)
    places = jnp.arange(SECTORS)[None, :]
    term_ids = jnp.arange(TERMS)[:, None]
    lower = (places % SD == 0) & (term_ids == 0)
    upper = (places % SD == SD - 1) & (term_ids == 1)
    offsets = jnp.where(lower, -SD, jnp.where(upper, SD, offsets))
    offsets = jnp.where(term_ids % TD == TD - 1, 0, offsets)
    return jnp.clip(places + offsets, 0, SECTORS - 1).astype(jnp.int32)


def plant(array, key, low, top_value):
    longest = array.shape.index(max(array.shape))
    spots = []
    for shift in (0, 1):
        where = [jax.random.randint(jax.random.fold_in(key, axis), (), 0, length) for axis, length in enumerate(array.shape)]
        where[longest] = (where[longest] + shift) % array.shape[longest]
        spots.append(tuple(where))
    return array.at[spots[0]].set(low).at[spots[1]].set(top_value)


def steps_of(key, dims, cuts, low, top_value):
    def one(dim, blocks):
        heights = jax.random.uniform(jax.random.fold_in(jax.random.fold_in(key, 6), dim), (blocks,), jnp.float32, low / len(cuts), top_value / len(cuts))
        return jnp.repeat(jnp.exp(heights), dims[dim] // blocks).reshape((-1,) + (1,) * (len(dims) - dim - 1))

    factor_of = one(*cuts[0])
    for cut in cuts[1:]:
        factor_of = factor_of * one(*cut)
    return factor_of


def gaussian(own_key, dims, spread, reach, cuts=(), dtype=jnp.bfloat16):
    factor_of = steps_of(own_key, dims, cuts, -0.22, 0.18) if cuts else 1.0
    array = jax.random.normal(own_key, dims, jnp.float32) * spread * factor_of
    return jnp.minimum(jnp.maximum(array, -reach), reach).astype(dtype)


def setup_inputs(seed: int = 0) -> dict:
    arg_keys = jax.random.split(jax.random.key(seed), 7)
    psi_start = gaussian(arg_keys[0], (SECTORS, DB, DB), 1.0, 6.0, ((0, 16),))
    left_env = draw_left_env(jax.random.fold_in(arg_keys[6], 71), 0)
    right_env = draw_right_env(jax.random.fold_in(arg_keys[6], 71), 0)
    connect = draw_connect(jax.random.fold_in(arg_keys[6], 71), 0)
    sector_dims = plant(jax.random.randint(arg_keys[4], (2, SECTORS), DB // 4, DB + 1), jax.random.fold_in(arg_keys[4], 1), DB // 4, DB).astype(jnp.int32)
    precond = jnp.clip(jnp.exp(math.log(4.0) - 2.0794415 * jax.random.uniform(arg_keys[5], (SECTORS, DB, DB), jnp.float32) ** steps_of(arg_keys[5], (SECTORS, DB, DB), ((0, 16),), -0.2, 0.2)), 0.5, 4.0).astype(jnp.bfloat16)
    return dict(psi_start=psi_start, left_env=left_env, right_env=right_env, connect=connect, sector_dims=sector_dims, precond=precond)


epsilon = 1e-06

def block_mask(sector_dims):
    row_ids = lax.broadcasted_iota(jnp.int32, (SECTORS, DB, DB), 1)
    col_ids = lax.broadcasted_iota(jnp.int32, (SECTORS, DB, DB), 2)
    keep = (row_ids < sector_dims[0][:, None, None]) & (col_ids < sector_dims[1][:, None, None])
    return keep.astype(jnp.float32)

def apply_terms(vector_b, left_env, right_env, connect, with_env):

    def one_term(total, pieces):
        left_one, right_one, source_one = pieces
        source = vector_b[source_one]
        half = jnp.einsum('sij,sjk->sik', left_one.astype(jnp.float32), source.astype(jnp.float32)).astype(jnp.bfloat16)
        total = total + jnp.einsum('sik,slk->sil', half.astype(jnp.float32), right_one.astype(jnp.float32))
        if with_env:
            env_one = jnp.einsum('sji,sjk->sik', vector_b.astype(jnp.float32), half.astype(jnp.float32)) * DB ** (-0.5)
            return (total, env_one.astype(jnp.bfloat16))
        return (total, None)
    return lax.scan(one_term, jnp.zeros((SECTORS, DB, DB), jnp.float32), (left_env, right_env, connect))

def reference(psi_start, left_env, right_env, connect, sector_dims, precond):
    mask = block_mask(sector_dims)
    entries = float(SECTORS * DB * DB)

    def inner(first, second):
        return jnp.sum(first * second) / entries
    vector = mask * psi_start.astype(jnp.float32)
    vector = vector / jnp.sqrt(inner(vector, vector) + epsilon)
    basis = [vector]
    sigmas = []
    new_env = None
    for which in range(3):
        vector_b = basis[which].astype(jnp.bfloat16)
        if which < 2:
            total, unused = apply_terms(vector_b, left_env, right_env, connect, False)
        else:
            total, new_env = apply_terms(vector_b, left_env, right_env, connect, True)
        sigma = total * mask
        sigmas.append(sigma)
        if which < 2:
            theta = inner(basis[which], sigma)
            corr = (sigma - theta * basis[which]) / precond.astype(jnp.float32)
            correlations = [inner(member, corr) for member in basis]
            for member, weight in zip(basis, correlations):
                corr = corr - weight * member
            corr = corr / jnp.sqrt(inner(corr, corr) + epsilon)
            basis.append(corr)
    projected = jnp.stack([jnp.stack([inner(basis[row], sigmas[col]) for col in range(3)]) for row in range(3)])
    return (projected, basis[2], new_env)
```

```python
import functools
import jax
import jax.numpy as jnp
from jax import lax
from jax.experimental import pallas as pl
from jax.experimental.pallas import tpu as pltpu
from jax.sharding import PartitionSpec as P

epsilon = 1e-06
MESH = pl.DeviceIdType.MESH
F32 = jnp.float32
BF16 = jnp.bfloat16


def fold(values):
    rows, width = values.shape
    total = values.reshape(rows // 8, 8, width).sum(axis=0)
    out = total[:, :128]
    for start in range(128, width, 128):
        out = out + total[:, start : start + 128]
    return out


def rounds_of(devices):
    out, stride = [], 1
    while stride < devices:
        radix = 4 if devices // stride % 4 == 0 else 2
        out.append((stride, radix))
        stride *= radix
    return out


def kernel(
    sizes, relays,
    dims, conn, psi_in, left_in, right_in, pre_in,
    proj, last, env,
    left, right, pre, psi, inverse_of, raw, far1, far2, far3, ext1, ext2, ext3, acc, stage, came, sig1, sig2, base1, base2,
    tile, slots, norm_tile, norm_slots,
    on_send, on_recv, off_send, off_recv, relay_send, share_send, share_recv, part_send, part_recv,
    sum_send, sum_recv, norm_send, norm_recv, load,
):
    pieces, devices, terms, blocks, width, entries = sizes
    share = width // pieces
    count = pieces * devices
    step = min(32, share)
    steps = share // step
    me_t = lax.axis_index("term")
    me_s = lax.axis_index("sector")
    me = me_t * devices + me_s
    first = me_s * blocks - blocks
    odd = lax.rem(me_s, 2)
    on_s = me_s + 1 - 2 * odd
    off_s = me_s - 1 + 2 * odd
    has_off = (off_s >= 0) & (off_s < devices)
    zero = jnp.zeros((8, 128), F32)
    rounds = rounds_of(devices)

    def order(k):
        return k + odd * (blocks - 1 - 2 * k)

    def turn(k):
        return blocks - 1 - k + odd * (2 * k - blocks + 1)

    def device_at(offset):
        other = lax.rem(me + offset, count)
        return (other // devices, lax.rem(other, devices))

    def term_at(offset):
        return lax.rem(me_t + offset, pieces)

    def rows_of(piece):
        return pl.ds(pl.multiple_of(piece * share, share), share)

    def part_rows(j):
        return rows_of(term_at(pieces - j))

    everything = pl.ds(0, width)

    def arrived(view, sem):
        pltpu.make_async_copy(view, view, sem).wait()

    loads = [
        pltpu.make_async_copy(source, target, load.at[i])
        for i, (source, target) in enumerate(
            ((psi_in, psi), (pre_in, pre), (left_in, left), (right_in, right))
        )
    ]
    loads[0].start()

    barrier = pltpu.get_barrier_semaphore()

    def greet(t, s):
        pl.semaphore_signal(barrier, inc=1, device_id=(t, s), device_id_type=MESH)

    def peers(stride, radix):
        digit = lax.rem(me_s // stride, radix)
        return digit, [
            me_s + (lax.rem(digit + d, radix) - digit) * stride for d in range(1, radix)
        ]

    greeted = pieces - 1
    for stride, radix in rounds:
        for other in peers(stride, radix)[1]:
            greet(me_t, other)
        greeted += radix - 1
    for j in range(1, pieces):
        greet(term_at(j), me_s)
    apart = has_off & (off_s // rounds[0][1] != me_s // rounds[0][1])

    @pl.when(apart)
    def _():
        greet(me_t, off_s)

    loads[0].wait()
    for one in loads[1:]:
        one.start()

    pl.semaphore_wait(barrier, greeted + apart.astype(jnp.int32))

    def on_copy(ref, s, j, rows):
        return pltpu.make_async_remote_copy(
            src_ref=ref.at[blocks + s, rows],
            dst_ref=ref.at[s + odd * 2 * blocks, rows],
            send_sem=on_send.at[j, s],
            recv_sem=on_recv.at[j, s],
            device_id=(me_t, on_s),
            device_id_type=MESH,
        )

    def on_arrived(ref, s, j, rows):
        arrived(ref.at[s + (1 - odd) * 2 * blocks, rows], on_recv.at[j, s])

    def off_copy(ref, far, s, j):
        return pltpu.make_async_remote_copy(
            src_ref=ref.at[blocks + s, part_rows(j)],
            dst_ref=far.at[s, part_rows(j)],
            send_sem=off_send.at[j, s],
            recv_sem=off_recv.at[j, s],
            device_id=(me_t, off_s),
            device_id_type=MESH,
        )

    def off_slot(s):
        return s + odd * 2 * blocks

    def off_arrived(far, s, j):
        arrived(far.at[s, part_rows(j)], off_recv.at[j, s])

    def relay_copy(far, s, j):
        return pltpu.make_async_remote_copy(
            src_ref=far.at[s, rows_of(me_t)],
            dst_ref=far.at[s, rows_of(me_t)],
            send_sem=relay_send.at[j - 1, s],
            recv_sem=off_recv.at[j, s],
            device_id=(term_at(j), me_s),
            device_id_type=MESH,
        )

    def relayed(k, span):
        return (k >= span[0]) & (k < span[1])

    def relay(far, k, span):
        @pl.when(has_off & relayed(k, span))
        def _():
            s = turn(k)
            off_arrived(far, s, 0)
            for j in range(1, pieces):
                relay_copy(far, s, j).start()

    def receive(far, k, span):
        s = turn(k)

        @pl.when(has_off & jnp.logical_not(relayed(k, span)))
        def _():
            off_arrived(far, s, 0)

        @pl.when(has_off)
        def _():
            for j in range(1, pieces):
                off_arrived(far, s, j)

    def sent(ref, far, span, whole):
        @pl.loop(0, blocks)
        def _(k):
            s = order(k)
            if whole:
                on_copy(ref, s, 0, everything).wait_send()
            else:
                for j in range(pieces):
                    on_copy(ref, s, j, part_rows(j)).wait_send()
                for offset in range(1, pieces):
                    share_copy(ref, s, offset, me_t).wait_send()

            @pl.when(has_off)
            def _():
                off_copy(ref, far, s, 0).wait_send()

            @pl.when(has_off & jnp.logical_not(relayed(k, span)))
            def _():
                for j in range(1, pieces):
                    off_copy(ref, far, s, j).wait_send()

            @pl.when(has_off & relayed(k, span))
            def _():
                for j in range(1, pieces):
                    relay_copy(far, turn(k), j).wait_send()

    def share_copy(ref, s, offset, piece):
        return pltpu.make_async_remote_copy(
            src_ref=ref.at[blocks + s, rows_of(piece)],
            dst_ref=ref.at[blocks + s, rows_of(piece)],
            send_sem=share_send.at[offset - 1, s],
            recv_sem=share_recv.at[offset - 1, s],
            device_id=(term_at(offset), me_s),
            device_id_type=MESH,
        )

    def part_copy(s, offset):
        return pltpu.make_async_remote_copy(
            src_ref=stage.at[offset - 1, s],
            dst_ref=came.at[offset - 1, s],
            send_sem=part_send.at[offset - 1, s],
            recv_sem=part_recv.at[offset - 1, s],
            device_id=(term_at(offset), me_s),
            device_id_type=MESH,
        )

    lane = lax.broadcasted_iota(jnp.int32, (1, 128), 1)

    def pack(tiles):
        packed = jnp.zeros((1, 128), F32)
        for i, one in enumerate(tiles):
            row = jnp.sum(one, axis=0, keepdims=True)
            packed = jnp.where(lane == i, jnp.sum(row, axis=1, keepdims=True), packed)
        return packed

    def sum_start(which, tiles):
        packed = pack(tiles)
        tile[which] = packed
        slots[which, me] = packed

        @pl.loop(1, count)
        def _(offset):
            pltpu.make_async_remote_copy(
                src_ref=tile.at[which],
                dst_ref=slots.at[which, me],
                send_sem=sum_send.at[which],
                recv_sem=sum_recv.at[which],
                device_id=device_at(offset),
                device_id_type=MESH,
            ).start()

    def sum_finish(which):
        others = slots.at[which, pl.ds(0, count - 1)]
        arrived(others, sum_recv.at[which])
        full = jnp.sum(slots[which], axis=0) / entries
        return lambda i: full[:, i : i + 1]

    def norm_start(i, packed):
        digit, others = peers(*rounds[i])
        norm_tile[i] = packed
        norm_slots[i, digit] = packed
        for other in others:
            pltpu.make_async_remote_copy(
                src_ref=norm_tile.at[i],
                dst_ref=norm_slots.at[i, digit],
                send_sem=norm_send.at[i],
                recv_sem=norm_recv.at[i],
                device_id=(me_t, other),
                device_id_type=MESH,
            ).start()

    def norm_finish(i):
        radix = rounds[i][1]
        arrived(norm_slots.at[i, pl.ds(0, radix - 1)], norm_recv.at[i])
        return jnp.sum(norm_slots[i, pl.ds(0, radix)], axis=0)

    starts = [k * step for k in range(steps)]
    strips = list(range(0, width, step))

    def own_rows(start):
        return pl.ds(pl.multiple_of(me_t * share + start, step), step)

    span0 = relays[0]

    def first_step(k, total):
        s = order(k)
        for start in strips:
            here = pl.ds(start, step)
            rows = lax.broadcasted_iota(jnp.int32, (step, width), 0) + start
            cols = lax.broadcasted_iota(jnp.int32, (step, width), 1)
            keep = (rows < dims[0, s]) & (cols < dims[1, s])
            v = jnp.where(keep, psi[s, here, :].astype(F32), 0.0)
            raw[blocks + s, here, :] = v.astype(BF16)
            total = total + fold(v * v)
        return total

    norm_start(0, pack([lax.fori_loop(0, blocks, first_step, zero)]))

    @pl.loop(0, blocks)
    def _(k):
        s = order(k)
        on_copy(raw, s, 0, everything).start()

        @pl.when(has_off)
        def _():
            off_copy(raw, far1, s, 0).start()

        @pl.when(has_off & jnp.logical_not(relayed(k, span0)))
        def _():
            for j in range(1, pieces):
                off_copy(raw, far1, s, j).start()

    loads[1].wait()

    @pl.loop(0, blocks)
    def _(s):
        for start in starts:
            inverse_of[s, pl.ds(start, step), :] = 1.0 / pre[s, own_rows(start), :].astype(F32)

    total = None
    for i in range(len(rounds)):
        total = norm_finish(i)
        if i + 1 < len(rounds):
            norm_start(i + 1, total)
        if i == 0:
            for k in range(relays[0][2]):
                relay(far1, k, span0)
    norm = total[:, 0:1] / entries
    scale = 1.0 / jnp.sqrt(norm + epsilon)

    def scaled(source, place, slot):
        for start in strips:
            here = pl.ds(start, step)
            ext1[slot, here, :] = (source[place, here, :].astype(F32) * scale).astype(BF16)

    @pl.loop(0, blocks)
    def _(s):
        scaled(raw, blocks + s, blocks + s)
        for start in starts:
            base1[s, pl.ds(start, step), :] = raw[blocks + s, own_rows(start), :].astype(F32) * scale

    @pl.loop(0, blocks)
    def _(k):
        s = turn(k)
        on_arrived(raw, s, 0, everything)
        slot = s + (1 - odd) * 2 * blocks
        scaled(raw, slot, slot)

    def product(ref, s, keep):
        halves = []
        for t in range(terms):
            source = ref[jnp.clip(conn[t, s] - first, 0, 3 * blocks - 1)]
            one = jnp.dot(left[t, s], source, preferred_element_type=F32).astype(BF16)
            halves.append(one)
            if keep:
                env[t, s] = one
        total = None
        for t in range(terms):
            one = lax.dot_general(
                halves[t], right[t, s], (((1,), (1,)), ((), ())), preferred_element_type=F32
            )
            total = one if total is None else total + one
        return total

    def take(ref, far, k, span, scaling):
        s = turn(k)
        relay(far, k + span[2], span)
        receive(far, k, span)

        @pl.when(has_off)
        def _():
            if scaling:
                scaled(far, s, off_slot(s))
            else:
                ref[off_slot(s)] = far[s]

    def apply(ref, far, span, scaling):
        @pl.loop(0, blocks)
        def _(k):
            take(ref, far, k, span, scaling)
            s = turn(k)
            acc[s] = product(ref, s, False)
            for offset in range(1, pieces):
                stage[offset - 1, s] = acc[s, rows_of(term_at(offset)), :].astype(BF16)
                part_copy(s, offset).start()

    def masked_sum(s, start):
        total = acc[s, own_rows(start), :]
        for offset in range(1, pieces):
            total = total + came[offset - 1, s, pl.ds(start, step), :].astype(F32)
        rows = lax.broadcasted_iota(jnp.int32, (step, width), 0) + (me_t * share + start)
        cols = lax.broadcasted_iota(jnp.int32, (step, width), 1)
        return jnp.where((rows < dims[0, s]) & (cols < dims[1, s]), total, 0.0)

    def divided(s, start):
        return inverse_of[s, pl.ds(start, step), :]

    def part_wait(s):
        for offset in range(1, pieces):
            part_copy(s, offset).wait()

    def spread(ref, far, out, corr_of, span):
        @pl.loop(0, blocks)
        def _(k):
            s = order(k)
            for start in starts:
                value = corr_of(s, start)
                out[s, pl.ds(start, step), :] = value
                ref[blocks + s, own_rows(start), :] = value.astype(BF16)

            for offset in range(1, pieces):
                share_copy(ref, s, offset, me_t).start()
            on_copy(ref, s, 0, part_rows(0)).start()

            @pl.when(has_off)
            def _():
                off_copy(ref, far, s, 0).start()

        @pl.loop(0, blocks)
        def _(k):
            s = order(k)
            for offset in range(1, pieces):
                arrived(ref.at[blocks + s, part_rows(offset)], share_recv.at[offset - 1, s])
                on_copy(ref, s, offset, part_rows(offset)).start()

                @pl.when(has_off & jnp.logical_not(relayed(k, span)))
                def _():
                    off_copy(ref, far, s, offset).start()

        for k in range(span[2]):
            relay(far, k, span)

    def settle(ref):
        @pl.loop(0, blocks)
        def _(k):
            s = turn(k)
            for j in range(pieces):
                on_arrived(ref, s, j, part_rows(j))

    loads[2].wait()
    loads[3].wait()
    apply(ext1, far1, span0, True)

    def sums1(k, totals):
        s = turn(k)
        part_wait(s)
        for start in starts:
            totals = sums1_rows(s, start, totals)
        return totals

    def sums1_rows(s, start, totals):
        here = pl.ds(start, step)
        sigma = masked_sum(s, start)
        sig1[s, here, :] = sigma
        inverse = divided(s, start)
        b1 = base1[s, here, :]
        r = sigma * inverse
        q = b1 * inverse
        pairs = [(b1, sigma), (b1, r), (b1, q), (r, r), (r, q), (q, q), (b1, b1)]
        return tuple(t + fold(x * y) for t, (x, y) in zip(totals, pairs))

    sum_start(0, lax.fori_loop(0, blocks, sums1, (zero,) * 7))
    sent(raw, far1, span0, True)
    got = sum_finish(0)
    theta1 = got(0)
    first_gram = got(6)
    weight = got(1) - theta1 * got(2)
    length = (
        (got(3) - 2.0 * theta1 * got(4) + theta1 * theta1 * got(5))
        - 2.0 * weight * weight
        + weight * weight * first_gram
    )
    scale1 = 1.0 / jnp.sqrt(jnp.maximum(length, 0.0) + epsilon)

    def corr1(s, start):
        here = pl.ds(start, step)
        b1 = base1[s, here, :]
        corr = (sig1[s, here, :] - theta1 * b1) * divided(s, start)
        return (corr - weight * b1) * scale1

    spread(ext2, far2, base2, corr1, relays[1])
    settle(ext2)
    apply(ext2, far2, relays[1], False)

    def sums2(k, totals):
        s = turn(k)
        part_wait(s)
        for start in starts:
            totals = sums2_rows(s, start, totals)
        return totals

    def sums2_rows(s, start, totals):
        here = pl.ds(start, step)
        sigma = masked_sum(s, start)
        sig2[s, here, :] = sigma
        inverse = divided(s, start)
        b1 = base1[s, here, :]
        b2 = base2[s, here, :]
        r = sigma * inverse
        q = b2 * inverse
        pairs = [
            (b2, sigma), (b1, r), (b2, r), (b1, q), (b2, q), (r, r), (r, q), (q, q),
            (b1, b2), (b2, b2), (b1, sigma), (b2, sig1[s, here, :]),
        ]
        return tuple(t + fold(x * y) for t, (x, y) in zip(totals, pairs))

    sum_start(1, lax.fori_loop(0, blocks, sums2, (zero,) * 12))
    sent(ext2, far2, relays[1], False)
    more = sum_finish(1)
    theta2 = more(0)
    weight1 = more(1) - theta2 * more(3)
    weight2 = more(2) - theta2 * more(4)
    length2 = (
        (more(5) - 2.0 * theta2 * more(6) + theta2 * theta2 * more(7))
        - 2.0 * (weight1 * weight1 + weight2 * weight2)
        + weight1 * weight1 * first_gram
        + 2.0 * weight1 * weight2 * more(8)
        + weight2 * weight2 * more(9)
    )
    scale2 = 1.0 / jnp.sqrt(jnp.maximum(length2, 0.0) + epsilon)

    def corr2(s, start):
        here = pl.ds(start, step)
        b1 = base1[s, here, :]
        b2 = base2[s, here, :]
        corr = (sig2[s, here, :] - theta2 * b2) * divided(s, start)
        return (corr - weight1 * b1 - weight2 * b2) * scale2

    def cross(s, totals):
        for start in starts:
            here = pl.ds(start, step)
            b3 = last[s, here, :]
            pairs = [(b3, sig1[s, here, :]), (b3, sig2[s, here, :])]
            totals = tuple(t + fold(x * y) for t, (x, y) in zip(totals, pairs))
        return totals

    spread(ext3, far3, last, corr2, relays[2])
    crossed = lax.fori_loop(0, blocks, cross, (zero,) * 2)
    settle(ext3)

    def sums3(k, totals):
        take(ext3, far3, k, relays[2], False)
        s = turn(k)
        acc[s] = product(ext3, s, True)

        for start in strips:
            here = pl.ds(start, step)
            sigma = acc[s, here, :]
            vectors = [ref[blocks + s, here, :].astype(F32) for ref in (ext1, ext2, ext3)]
            totals = tuple(t + fold(v * sigma) for t, v in zip(totals, vectors))
        return totals

    sum_start(2, list(lax.fori_loop(0, blocks, sums3, (zero,) * 3)) + list(crossed))

    @pl.loop(0, blocks)
    def _(s):
        own = ext3[blocks + s]
        for t in range(terms):
            new = lax.dot_general(
                own, env[t, s], (((0,), (0,)), ((), ())), preferred_element_type=F32
            )
            env[t, s] = (new * width ** (-0.5)).astype(BF16)

    sent(ext3, far3, relays[2], False)
    end = sum_finish(2)
    cells = [
        [theta1, more(10), end(0)],
        [more(11), theta2, end(1)],
        [end(3), end(4), end(2)],
    ]
    row = lax.broadcasted_iota(jnp.int32, (8, 128), 0)
    col = lax.broadcasted_iota(jnp.int32, (8, 128), 1)
    out = zero
    for i in range(3):
        for j in range(3):
            out = jnp.where((row == i) & (col == j), cells[i][j], out)
    proj[...] = out

    for which in range(3):
        arrived(slots.at[which, pl.ds(0, count - 1)], sum_send.at[which])
    for i, (stride, radix) in enumerate(rounds):
        arrived(norm_slots.at[i, pl.ds(0, radix - 1)], norm_send.at[i])


def write_kernel(proj, last, env, proj_out, last_out, env_out, sem):
    copies = [
        pltpu.make_async_copy(last, last_out, sem.at[0]),
        pltpu.make_async_copy(env, env_out, sem.at[1]),
    ]
    for one in copies:
        one.start()
    proj_out[...] = proj[:3, :3]
    for one in copies:
        one.wait()


def write(proj, last, env):
    vmem = pl.BlockSpec(memory_space=pltpu.VMEM)
    anywhere = pl.BlockSpec(memory_space=pl.ANY)
    hbm = pl.BlockSpec(memory_space=pltpu.HBM)
    return pl.pallas_call(
        write_kernel,
        name="write",
        out_shape=(
            jax.ShapeDtypeStruct((3, 3), F32),
            jax.ShapeDtypeStruct(last.shape, F32),
            jax.ShapeDtypeStruct(env.shape, BF16),
        ),
        in_specs=[vmem, anywhere, anywhere],
        out_specs=(vmem, hbm, hbm),
        scratch_shapes=[pltpu.SemaphoreType.DMA((2,))],
        compiler_params=pltpu.CompilerParams(vmem_limit_bytes=12 * 1024 * 1024),
    )(proj, last, env)


RELAYS = ((0, 4, 2), (7, 8, 4), (4, 8, 4))


def on_device(psi, left, right, connect, sector_dims, precond):
    blocks, width = psi.shape[0], psi.shape[1]
    terms = left.shape[0]
    pieces, devices = lax.axis_size("term"), lax.axis_size("sector")
    count = pieces * devices
    share = width // pieces
    entries = float(blocks * devices * width * width)
    sizes = (pieces, devices, terms, blocks, width, entries)
    others = max(pieces - 1, 1)
    rounds = len(rounds_of(devices))
    dma = pltpu.SemaphoreType.DMA
    vmem = pl.BlockSpec(memory_space=pltpu.VMEM)
    smem = pl.BlockSpec(memory_space=pltpu.SMEM)
    hbm = pl.BlockSpec(memory_space=pltpu.HBM)
    operands = [
        pltpu.with_memory_space_constraint(one, pltpu.HBM)
        for one in (sector_dims, connect, psi, left, right, precond)
    ]
    proj, last, env = pl.pallas_call(
        functools.partial(kernel, sizes, RELAYS),
        name="davidson",
        out_shape=(
            jax.ShapeDtypeStruct((8, 128), F32),
            pltpu.VMEM((blocks, share, width), F32),
            pltpu.VMEM((terms, blocks, width, width), BF16),
        ),
        in_specs=[smem, smem, hbm, hbm, hbm, hbm],
        out_specs=(vmem, vmem, vmem),
        scratch_shapes=[
            pltpu.VMEM((terms, blocks, width, width), BF16),
            pltpu.VMEM((terms, blocks, width, width), BF16),
            pltpu.VMEM((blocks, width, width), BF16),
            pltpu.VMEM((blocks, width, width), BF16),
            pltpu.VMEM((blocks, share, width), F32),
            pltpu.VMEM((3 * blocks, width, width), BF16),
            pltpu.VMEM((blocks, width, width), BF16),
            pltpu.VMEM((blocks, width, width), BF16),
            pltpu.VMEM((blocks, width, width), BF16),
            pltpu.VMEM((3 * blocks, width, width), BF16),
            pltpu.VMEM((3 * blocks, width, width), BF16),
            pltpu.VMEM((3 * blocks, width, width), BF16),
            pltpu.VMEM((blocks, width, width), F32),
            pltpu.VMEM((others, blocks, share, width), BF16),
            pltpu.VMEM((others, blocks, share, width), BF16),
            pltpu.VMEM((blocks, share, width), F32),
            pltpu.VMEM((blocks, share, width), F32),
            pltpu.VMEM((blocks, share, width), F32),
            pltpu.VMEM((blocks, share, width), F32),
            pltpu.VMEM((3, 1, 128), F32),
            pltpu.VMEM((3, count, 1, 128), F32),
            pltpu.VMEM((rounds, 1, 128), F32),
            pltpu.VMEM((rounds, 4, 1, 128), F32),
            dma((pieces, blocks)),
            dma((pieces, blocks)),
            dma((pieces, blocks)),
            dma((pieces, blocks)),
            dma((others, blocks)),
            dma((others, blocks)),
            dma((others, blocks)),
            dma((others, blocks)),
            dma((others, blocks)),
            dma((3,)),
            dma((3,)),
            dma((rounds,)),
            dma((rounds,)),
            dma((4,)),
        ],
        compiler_params=pltpu.CompilerParams(
            collective_id=0, has_side_effects=True, vmem_limit_bytes=48 * 1024 * 1024
        ),
    )(*operands)
    return write(proj, last, env)


def solution(mesh):
    placed = (
        P("sector", None, None),
        P("term", "sector", None, None),
        P("term", "sector", None, None),
        P("term", "sector"),
        P(None, "sector"),
        P("sector", None, None),
    )
    return jax.shard_map(
        on_device,
        mesh=mesh,
        in_specs=placed,
        out_specs=(P(), P("sector", "term", None), P("term", "sector", None, None)),
        check_vma=False,
    )
```

```python
import functools
import jax
import jax.numpy as jnp
from jax import lax
from jax.experimental import pallas as pl
from jax.experimental.pallas import tpu as pltpu
from jax.sharding import PartitionSpec as P

epsilon = 1e-06
MESH = pl.DeviceIdType.MESH
F32 = jnp.float32
BF16 = jnp.bfloat16


def fold(values):
    rows, width = values.shape
    total = values.reshape(rows // 8, 8, width).sum(axis=0)
    out = total[:, :128]
    for start in range(128, width, 128):
        out = out + total[:, start : start + 128]
    return out


def rounds_of(devices):
    out, stride = [], 1
    while stride < devices:
        radix = 4 if devices // stride % 4 == 0 else 2
        out.append((stride, radix))
        stride *= radix
    return out


def kernel(
    sizes, relays,
    dims, conn, psi_in, left_in, right_in, pre_in,
    proj, last, env,
    left, right, pre, psi, inverse_of, raw, far1, far2, far3, ext1, ext2, ext3, acc, stage, came, mine, given, other2, sig1, sig2, base1, base2,
    tile, slots, term_tile, term_slots, norm_tile, norm_slots,
    on_send, on_recv, off_send, off_recv, relay_send, share_send, share_recv, mine_send, mine_recv, part_send, part_recv,
    sum_send, sum_recv, term_send, term_recv, norm_send, norm_recv, load,
):
    pieces, devices, terms, blocks, width, entries = sizes
    share = width // pieces
    count = pieces * devices
    step = min(32, share)
    steps = share // step
    me_t = lax.axis_index("term")
    me_s = lax.axis_index("sector")
    me = me_t * devices + me_s
    first = me_s * blocks - blocks
    paired = pieces == 2
    odd = lax.rem(me_s, 2)
    on_s = me_s + 1 - 2 * odd
    off_s = me_s - 1 + 2 * odd
    has_off = (off_s >= 0) & (off_s < devices)
    zero = jnp.zeros((8, 128), F32)
    rounds = rounds_of(devices)

    def order(k):
        return k + odd * (blocks - 1 - 2 * k)

    def turn(k):
        return blocks - 1 - k + odd * (2 * k - blocks + 1)

    def device_at(offset):
        other = lax.rem(me + offset, count)
        return (other // devices, lax.rem(other, devices))

    def term_at(offset):
        return lax.rem(me_t + offset, pieces)

    def rows_of(piece):
        return pl.ds(pl.multiple_of(piece * share, share), share)

    def part_rows(j):
        return rows_of(term_at(pieces - j))

    everything = pl.ds(0, width)

    def arrived(view, sem):
        pltpu.make_async_copy(view, view, sem).wait()

    loads = [
        pltpu.make_async_copy(source, target, load.at[i])
        for i, (source, target) in enumerate(
            ((psi_in, psi), (pre_in, pre), (left_in, left), (right_in, right))
        )
    ]
    loads[0].start()

    barrier = pltpu.get_barrier_semaphore()

    def greet(t, s):
        pl.semaphore_signal(barrier, inc=1, device_id=(t, s), device_id_type=MESH)

    def peers(stride, radix):
        digit = lax.rem(me_s // stride, radix)
        return digit, [
            me_s + (lax.rem(digit + d, radix) - digit) * stride for d in range(1, radix)
        ]

    greeted = pieces - 1
    for stride, radix in rounds:
        for other in peers(stride, radix)[1]:
            greet(me_t, other)
        greeted += radix - 1
    for j in range(1, pieces):
        greet(term_at(j), me_s)
    apart = has_off & (off_s // rounds[0][1] != me_s // rounds[0][1])

    @pl.when(apart)
    def _():
        greet(me_t, off_s)

    loads[0].wait()
    for one in loads[1:]:
        one.start()


    def on_copy(ref, s, j, rows):
        return pltpu.make_async_remote_copy(
            src_ref=ref.at[blocks + s, rows],
            dst_ref=ref.at[s + odd * 2 * blocks, rows],
            send_sem=on_send.at[j, s],
            recv_sem=on_recv.at[j, s],
            device_id=(me_t, on_s),
            device_id_type=MESH,
        )

    def on_arrived(ref, s, j, rows):
        arrived(ref.at[s + (1 - odd) * 2 * blocks, rows], on_recv.at[j, s])

    def off_copy(ref, far, s, j):
        return pltpu.make_async_remote_copy(
            src_ref=ref.at[blocks + s, part_rows(j)],
            dst_ref=far.at[s, part_rows(j)],
            send_sem=off_send.at[j, s],
            recv_sem=off_recv.at[j, s],
            device_id=(me_t, off_s),
            device_id_type=MESH,
        )

    def off_slot(s):
        return s + odd * 2 * blocks

    def off_arrived(far, s, j):
        arrived(far.at[s, part_rows(j)], off_recv.at[j, s])

    def relay_copy(far, s, j):
        return pltpu.make_async_remote_copy(
            src_ref=far.at[s, rows_of(me_t)],
            dst_ref=far.at[s, rows_of(me_t)],
            send_sem=relay_send.at[j - 1, s],
            recv_sem=off_recv.at[j, s],
            device_id=(term_at(j), me_s),
            device_id_type=MESH,
        )

    def relayed(k, span):
        return (k >= span[0]) & (k < span[1])

    def relay(far, k, span):
        @pl.when(has_off & relayed(k, span))
        def _():
            s = turn(k)
            off_arrived(far, s, 0)
            for j in range(1, pieces):
                relay_copy(far, s, j).start()

    def receive(far, k, span):
        s = turn(k)

        @pl.when(has_off & jnp.logical_not(relayed(k, span)))
        def _():
            off_arrived(far, s, 0)

        @pl.when(has_off)
        def _():
            for j in range(1, pieces):
                off_arrived(far, s, j)

    def sent(ref, far, span, whole):
        @pl.loop(0, blocks)
        def _(k):
            s = order(k)
            if whole:
                on_copy(ref, s, 0, everything).wait_send()
            else:
                for j in range(pieces):
                    on_copy(ref, s, j, part_rows(j)).wait_send()
                if not paired:
                    for offset in range(1, pieces):
                        share_copy(ref, s, offset, me_t).wait_send()

            @pl.when(has_off)
            def _():
                off_copy(ref, far, s, 0).wait_send()

            @pl.when(has_off & jnp.logical_not(relayed(k, span)))
            def _():
                for j in range(1, pieces):
                    off_copy(ref, far, s, j).wait_send()

            @pl.when(has_off & relayed(k, span))
            def _():
                for j in range(1, pieces):
                    relay_copy(far, turn(k), j).wait_send()

    def share_copy(ref, s, offset, piece):
        return pltpu.make_async_remote_copy(
            src_ref=ref.at[blocks + s, rows_of(piece)],
            dst_ref=ref.at[blocks + s, rows_of(piece)],
            send_sem=share_send.at[offset - 1, s],
            recv_sem=share_recv.at[offset - 1, s],
            device_id=(term_at(offset), me_s),
            device_id_type=MESH,
        )

    def mine_copy(which, s):
        return pltpu.make_async_remote_copy(
            src_ref=mine.at[s],
            dst_ref=given.at[which, s],
            send_sem=mine_send.at[which, s],
            recv_sem=mine_recv.at[which, s],
            device_id=(term_at(1), me_s),
            device_id_type=MESH,
        )

    def part_copy(s, offset):
        return pltpu.make_async_remote_copy(
            src_ref=stage.at[offset - 1, s],
            dst_ref=came.at[offset - 1, s],
            send_sem=part_send.at[offset - 1, s],
            recv_sem=part_recv.at[offset - 1, s],
            device_id=(term_at(offset), me_s),
            device_id_type=MESH,
        )

    lane = lax.broadcasted_iota(jnp.int32, (1, 128), 1)

    def pack(tiles):
        packed = jnp.zeros((1, 128), F32)
        for i, one in enumerate(tiles):
            row = jnp.sum(one, axis=0, keepdims=True)
            packed = jnp.where(lane == i, jnp.sum(row, axis=1, keepdims=True), packed)
        return packed

    def term_start(which, tiles):
        packed = pack(tiles)
        term_tile[which] = packed
        term_slots[which, me_t] = packed
        for offset in range(1, pieces):
            pltpu.make_async_remote_copy(
                src_ref=term_tile.at[which],
                dst_ref=term_slots.at[which, me_t],
                send_sem=term_send.at[which],
                recv_sem=term_recv.at[which],
                device_id=(term_at(offset), me_s),
                device_id_type=MESH,
            ).start()

    def sector_start(which):
        arrived(term_slots.at[which, pl.ds(0, pieces - 1)], term_recv.at[which])
        packed = jnp.sum(term_slots[which], axis=0)
        tile[which] = packed
        slots[which, me_s] = packed

        @pl.loop(1, devices)
        def _(offset):
            pltpu.make_async_remote_copy(
                src_ref=tile.at[which],
                dst_ref=slots.at[which, me_s],
                send_sem=sum_send.at[which],
                recv_sem=sum_recv.at[which],
                device_id=(me_t, lax.rem(me_s + offset, devices)),
                device_id_type=MESH,
            ).start()

    def sum_start(which, tiles):
        packed = pack(tiles)
        tile[which] = packed
        slots[which, me] = packed

        @pl.loop(1, count)
        def _(offset):
            pltpu.make_async_remote_copy(
                src_ref=tile.at[which],
                dst_ref=slots.at[which, me],
                send_sem=sum_send.at[which],
                recv_sem=sum_recv.at[which],
                device_id=device_at(offset),
                device_id_type=MESH,
            ).start()

    def sum_finish(which, members):
        others = slots.at[which, pl.ds(0, members - 1)]
        arrived(others, sum_recv.at[which])
        full = jnp.sum(slots[which, pl.ds(0, members)], axis=0) / entries
        return lambda i: full[:, i : i + 1]

    def norm_start(i, packed):
        digit, others = peers(*rounds[i])
        norm_tile[i] = packed
        norm_slots[i, digit] = packed
        for other in others:
            pltpu.make_async_remote_copy(
                src_ref=norm_tile.at[i],
                dst_ref=norm_slots.at[i, digit],
                send_sem=norm_send.at[i],
                recv_sem=norm_recv.at[i],
                device_id=(me_t, other),
                device_id_type=MESH,
            ).start()

    def norm_finish(i):
        radix = rounds[i][1]
        arrived(norm_slots.at[i, pl.ds(0, radix - 1)], norm_recv.at[i])
        return jnp.sum(norm_slots[i, pl.ds(0, radix)], axis=0)

    starts = [k * step for k in range(steps)]
    strips = list(range(0, width, step))

    def own_rows(start):
        return pl.ds(pl.multiple_of(me_t * share + start, step), step)

    span0 = relays[0]

    def first_step(k, total):
        s = order(k)
        for start in strips:
            here = pl.ds(start, step)
            rows = lax.broadcasted_iota(jnp.int32, (step, width), 0) + start
            cols = lax.broadcasted_iota(jnp.int32, (step, width), 1)
            keep = (rows < dims[0, s]) & (cols < dims[1, s])
            v = jnp.where(keep, psi[s, here, :].astype(F32), 0.0)
            raw[blocks + s, here, :] = v.astype(BF16)
            total = total + fold(v * v)
        return total

    own_norm = pack([lax.fori_loop(0, blocks, first_step, zero)])
    pl.semaphore_wait(barrier, greeted + apart.astype(jnp.int32))
    norm_start(0, own_norm)

    @pl.loop(0, blocks)
    def _(k):
        s = order(k)
        on_copy(raw, s, 0, everything).start()

        @pl.when(has_off)
        def _():
            off_copy(raw, far1, s, 0).start()

        @pl.when(has_off & jnp.logical_not(relayed(k, span0)))
        def _():
            for j in range(1, pieces):
                off_copy(raw, far1, s, j).start()

    loads[1].wait()

    @pl.loop(0, blocks)
    def _(s):
        for start in strips:
            here = pl.ds(start, step)
            inverse_of[s, here, :] = 1.0 / pre[s, here, :].astype(F32)

    total = None
    for i in range(len(rounds)):
        total = norm_finish(i)
        if i + 1 < len(rounds):
            norm_start(i + 1, total)
        if i == 0:
            for k in range(relays[0][2]):
                relay(far1, k, span0)
    norm = total[:, 0:1] / entries
    scale = 1.0 / jnp.sqrt(norm + epsilon)

    def scaled(source, place, slot):
        for start in strips:
            here = pl.ds(start, step)
            ext1[slot, here, :] = (source[place, here, :].astype(F32) * scale).astype(BF16)

    @pl.loop(0, blocks)
    def _(s):
        scaled(raw, blocks + s, blocks + s)
        for start in starts:
            base1[s, pl.ds(start, step), :] = raw[blocks + s, own_rows(start), :].astype(F32) * scale

    @pl.loop(0, blocks)
    def _(k):
        s = turn(k)
        on_arrived(raw, s, 0, everything)
        slot = s + (1 - odd) * 2 * blocks
        scaled(raw, slot, slot)

    def product(ref, s, keep):
        halves = []
        for t in range(terms):
            source = ref[jnp.clip(conn[t, s] - first, 0, 3 * blocks - 1)]
            one = jnp.dot(left[t, s], source, preferred_element_type=F32).astype(BF16)
            halves.append(one)
            if keep:
                env[t, s] = one
        total = None
        for t in range(terms):
            one = lax.dot_general(
                halves[t], right[t, s], (((1,), (1,)), ((), ())), preferred_element_type=F32
            )
            total = one if total is None else total + one
        return total

    def take(ref, far, k, span, scaling):
        s = turn(k)
        relay(far, k + span[2], span)
        receive(far, k, span)

        @pl.when(has_off)
        def _():
            if scaling:
                scaled(far, s, off_slot(s))
            else:
                ref[off_slot(s)] = far[s]

    def apply(ref, far, span, scaling):
        @pl.loop(0, blocks)
        def _(k):
            take(ref, far, k, span, scaling)
            s = turn(k)
            acc[s] = product(ref, s, False)
            for offset in range(1, pieces):
                stage[offset - 1, s] = acc[s, rows_of(term_at(offset)), :].astype(BF16)
                part_copy(s, offset).start()

    def masked(s, base, total):
        rows = lax.broadcasted_iota(jnp.int32, (step, width), 0) + base
        cols = lax.broadcasted_iota(jnp.int32, (step, width), 1)
        return jnp.where((rows < dims[0, s]) & (cols < dims[1, s]), total, 0.0)

    def masked_sum(s, start):
        total = acc[s, own_rows(start), :]
        for offset in range(1, pieces):
            total = total + came[offset - 1, s, pl.ds(start, step), :].astype(F32)
        return masked(s, me_t * share + start, total)

    def other_rows(start):
        return pl.ds(pl.multiple_of(term_at(1) * share + start, step), step)

    def other_sum(which, s, start):
        total = acc[s, other_rows(start), :] + given[which, s, pl.ds(start, step), :].astype(F32)
        return masked(s, term_at(1) * share + start, total)

    def give(which):
        if not paired:
            return

        @pl.loop(0, blocks)
        def _(k):
            s = order(k)
            mine[s] = acc[s, rows_of(me_t), :].astype(BF16)
            mine_copy(which, s).start()

    def divided(s, start):
        return inverse_of[s, own_rows(start), :]

    def part_wait(s):
        for offset in range(1, pieces):
            part_copy(s, offset).wait()

    def spread(which, ref, far, out, corr_of, other_of, span):
        @pl.loop(0, blocks)
        def _(k):
            s = order(k)
            for start in starts:
                value = corr_of(s, start)
                out[s, pl.ds(start, step), :] = value
                ref[blocks + s, own_rows(start), :] = value.astype(BF16)

            if not paired:
                for offset in range(1, pieces):
                    share_copy(ref, s, offset, me_t).start()
            on_copy(ref, s, 0, part_rows(0)).start()

            @pl.when(has_off)
            def _():
                off_copy(ref, far, s, 0).start()

            if paired:
                finish_block(which, ref, far, other_of, span, k)

        if not paired:

            @pl.loop(0, blocks)
            def _(k):
                finish_block(which, ref, far, other_of, span, k)

        for k in range(span[2]):
            relay(far, k, span)

    def finish_block(which, ref, far, other_of, span, k):
        s = order(k)
        if paired:
            mine_copy(which, s).wait()
            for start in starts:
                value = other_of(s, start, other_sum(which, s, start))
                ref[blocks + s, other_rows(start), :] = value.astype(BF16)
        for offset in range(1, pieces):
            if not paired:
                arrived(ref.at[blocks + s, part_rows(offset)], share_recv.at[offset - 1, s])
            on_copy(ref, s, offset, part_rows(offset)).start()

            @pl.when(has_off & jnp.logical_not(relayed(k, span)))
            def _():
                off_copy(ref, far, s, offset).start()

    def settle(ref):
        @pl.loop(0, blocks)
        def _(k):
            s = turn(k)
            for j in range(pieces):
                on_arrived(ref, s, j, part_rows(j))

    loads[2].wait()
    loads[3].wait()
    apply(ext1, far1, span0, True)

    def sums1(k, totals):
        s = turn(k)
        part_wait(s)
        for start in starts:
            totals = sums1_rows(s, start, totals)
        return totals

    def sums1_rows(s, start, totals):
        here = pl.ds(start, step)
        sigma = masked_sum(s, start)
        sig1[s, here, :] = sigma
        inverse = divided(s, start)
        b1 = base1[s, here, :]
        r = sigma * inverse
        q = b1 * inverse
        pairs = [(b1, sigma), (b1, r), (b1, q), (r, r), (r, q), (q, q), (b1, b1)]
        return tuple(t + fold(x * y) for t, (x, y) in zip(totals, pairs))

    term_start(0, lax.fori_loop(0, blocks, sums1, (zero,) * 7))
    give(0)
    sector_start(0)
    sent(raw, far1, span0, True)
    got = sum_finish(0, devices)
    theta1 = got(0)
    first_gram = got(6)
    weight = got(1) - theta1 * got(2)
    length = (
        (got(3) - 2.0 * theta1 * got(4) + theta1 * theta1 * got(5))
        - 2.0 * weight * weight
        + weight * weight * first_gram
    )
    scale1 = 1.0 / jnp.sqrt(jnp.maximum(length, 0.0) + epsilon)

    def corr1(s, start):
        here = pl.ds(start, step)
        b1 = base1[s, here, :]
        corr = (sig1[s, here, :] - theta1 * b1) * divided(s, start)
        return (corr - weight * b1) * scale1

    def first_other(s, start):
        return raw[blocks + s, other_rows(start), :].astype(F32) * scale

    def other1(s, start, sigma):
        b1 = first_other(s, start)
        corr = (sigma - theta1 * b1) * inverse_of[s, other_rows(start), :]
        value = (corr - weight * b1) * scale1
        other2[s, pl.ds(start, step), :] = value
        return value

    spread(0, ext2, far2, base2, corr1, other1, relays[1])
    settle(ext2)
    apply(ext2, far2, relays[1], False)

    def sums2(k, totals):
        s = turn(k)
        part_wait(s)
        for start in starts:
            totals = sums2_rows(s, start, totals)
        return totals

    def sums2_rows(s, start, totals):
        here = pl.ds(start, step)
        sigma = masked_sum(s, start)
        sig2[s, here, :] = sigma
        inverse = divided(s, start)
        b1 = base1[s, here, :]
        b2 = base2[s, here, :]
        r = sigma * inverse
        q = b2 * inverse
        pairs = [
            (b2, sigma), (b1, r), (b2, r), (b1, q), (b2, q), (r, r), (r, q), (q, q),
            (b1, b2), (b2, b2), (b1, sigma), (b2, sig1[s, here, :]),
        ]
        return tuple(t + fold(x * y) for t, (x, y) in zip(totals, pairs))

    term_start(1, lax.fori_loop(0, blocks, sums2, (zero,) * 12))
    give(1)
    sector_start(1)
    sent(ext2, far2, relays[1], False)
    more = sum_finish(1, devices)
    theta2 = more(0)
    weight1 = more(1) - theta2 * more(3)
    weight2 = more(2) - theta2 * more(4)
    length2 = (
        (more(5) - 2.0 * theta2 * more(6) + theta2 * theta2 * more(7))
        - 2.0 * (weight1 * weight1 + weight2 * weight2)
        + weight1 * weight1 * first_gram
        + 2.0 * weight1 * weight2 * more(8)
        + weight2 * weight2 * more(9)
    )
    scale2 = 1.0 / jnp.sqrt(jnp.maximum(length2, 0.0) + epsilon)

    def corr2(s, start):
        here = pl.ds(start, step)
        b1 = base1[s, here, :]
        b2 = base2[s, here, :]
        corr = (sig2[s, here, :] - theta2 * b2) * divided(s, start)
        return (corr - weight1 * b1 - weight2 * b2) * scale2

    def other2_of(s, start, sigma):
        b1 = first_other(s, start)
        b2 = other2[s, pl.ds(start, step), :]
        corr = (sigma - theta2 * b2) * inverse_of[s, other_rows(start), :]
        return (corr - weight1 * b1 - weight2 * b2) * scale2

    def cross(s, totals):
        for start in starts:
            here = pl.ds(start, step)
            b3 = last[s, here, :]
            pairs = [(b3, sig1[s, here, :]), (b3, sig2[s, here, :])]
            totals = tuple(t + fold(x * y) for t, (x, y) in zip(totals, pairs))
        return totals

    spread(1, ext3, far3, last, corr2, other2_of, relays[2])
    crossed = lax.fori_loop(0, blocks, cross, (zero,) * 2)
    settle(ext3)

    def sums3(k, totals):
        take(ext3, far3, k, relays[2], False)
        s = turn(k)
        acc[s] = product(ext3, s, True)

        for start in strips:
            here = pl.ds(start, step)
            sigma = acc[s, here, :]
            vectors = [ref[blocks + s, here, :].astype(F32) for ref in (ext1, ext2, ext3)]
            totals = tuple(t + fold(v * sigma) for t, v in zip(totals, vectors))
        return totals

    sum_start(2, list(lax.fori_loop(0, blocks, sums3, (zero,) * 3)) + list(crossed))

    @pl.loop(0, blocks)
    def _(s):
        own = ext3[blocks + s]
        for t in range(terms):
            new = lax.dot_general(
                own, env[t, s], (((0,), (0,)), ((), ())), preferred_element_type=F32
            )
            env[t, s] = (new * width ** (-0.5)).astype(BF16)

    sent(ext3, far3, relays[2], False)
    end = sum_finish(2, count)
    cells = [
        [theta1, more(10), end(0)],
        [more(11), theta2, end(1)],
        [end(3), end(4), end(2)],
    ]
    row = lax.broadcasted_iota(jnp.int32, (8, 128), 0)
    col = lax.broadcasted_iota(jnp.int32, (8, 128), 1)
    out = zero
    for i in range(3):
        for j in range(3):
            out = jnp.where((row == i) & (col == j), cells[i][j], out)
    proj[...] = out

    for which, members in enumerate((devices, devices, count)):
        arrived(slots.at[which, pl.ds(0, members - 1)], sum_send.at[which])
    for which in range(2):
        arrived(term_slots.at[which, pl.ds(0, pieces - 1)], term_send.at[which])
    for i, (stride, radix) in enumerate(rounds):
        arrived(norm_slots.at[i, pl.ds(0, radix - 1)], norm_send.at[i])


def write_kernel(proj, last, env, proj_out, last_out, env_out, sem):
    copies = [
        pltpu.make_async_copy(last, last_out, sem.at[0]),
        pltpu.make_async_copy(env, env_out, sem.at[1]),
    ]
    for one in copies:
        one.start()
    proj_out[...] = proj[:3, :3]
    for one in copies:
        one.wait()


def write(proj, last, env):
    vmem = pl.BlockSpec(memory_space=pltpu.VMEM)
    anywhere = pl.BlockSpec(memory_space=pl.ANY)
    hbm = pl.BlockSpec(memory_space=pltpu.HBM)
    return pl.pallas_call(
        write_kernel,
        name="write",
        out_shape=(
            jax.ShapeDtypeStruct((3, 3), F32),
            jax.ShapeDtypeStruct(last.shape, F32),
            jax.ShapeDtypeStruct(env.shape, BF16),
        ),
        in_specs=[vmem, anywhere, anywhere],
        out_specs=(vmem, hbm, hbm),
        scratch_shapes=[pltpu.SemaphoreType.DMA((2,))],
        compiler_params=pltpu.CompilerParams(vmem_limit_bytes=12 * 1024 * 1024),
    )(proj, last, env)


RELAYS = ((0, 4, 4), (0, 2, 2), (0, 5, 3))


def on_device(psi, left, right, connect, sector_dims, precond):
    blocks, width = psi.shape[0], psi.shape[1]
    terms = left.shape[0]
    pieces, devices = lax.axis_size("term"), lax.axis_size("sector")
    count = pieces * devices
    share = width // pieces
    entries = float(blocks * devices * width * width)
    sizes = (pieces, devices, terms, blocks, width, entries)
    others = max(pieces - 1, 1)
    rounds = len(rounds_of(devices))
    dma = pltpu.SemaphoreType.DMA
    vmem = pl.BlockSpec(memory_space=pltpu.VMEM)
    smem = pl.BlockSpec(memory_space=pltpu.SMEM)
    hbm = pl.BlockSpec(memory_space=pltpu.HBM)
    operands = [
        pltpu.with_memory_space_constraint(one, pltpu.HBM)
        for one in (sector_dims, connect, psi, left, right, precond)
    ]
    proj, last, env = pl.pallas_call(
        functools.partial(kernel, sizes, RELAYS),
        name="davidson",
        out_shape=(
            jax.ShapeDtypeStruct((8, 128), F32),
            pltpu.VMEM((blocks, share, width), F32),
            pltpu.VMEM((terms, blocks, width, width), BF16),
        ),
        in_specs=[smem, smem, hbm, hbm, hbm, hbm],
        out_specs=(vmem, vmem, vmem),
        scratch_shapes=[
            pltpu.VMEM((terms, blocks, width, width), BF16),
            pltpu.VMEM((terms, blocks, width, width), BF16),
            pltpu.VMEM((blocks, width, width), BF16),
            pltpu.VMEM((blocks, width, width), BF16),
            pltpu.VMEM((blocks, width, width), F32),
            pltpu.VMEM((3 * blocks, width, width), BF16),
            pltpu.VMEM((blocks, width, width), BF16),
            pltpu.VMEM((blocks, width, width), BF16),
            pltpu.VMEM((blocks, width, width), BF16),
            pltpu.VMEM((3 * blocks, width, width), BF16),
            pltpu.VMEM((3 * blocks, width, width), BF16),
            pltpu.VMEM((3 * blocks, width, width), BF16),
            pltpu.VMEM((blocks, width, width), F32),
            pltpu.VMEM((others, blocks, share, width), BF16),
            pltpu.VMEM((others, blocks, share, width), BF16),
            pltpu.VMEM((blocks, share, width), BF16),
            pltpu.VMEM((2, blocks, share, width), BF16),
            pltpu.VMEM((blocks, share, width), F32),
            pltpu.VMEM((blocks, share, width), F32),
            pltpu.VMEM((blocks, share, width), F32),
            pltpu.VMEM((blocks, share, width), F32),
            pltpu.VMEM((blocks, share, width), F32),
            pltpu.VMEM((3, 1, 128), F32),
            pltpu.VMEM((3, count, 1, 128), F32),
            pltpu.VMEM((2, 1, 128), F32),
            pltpu.VMEM((2, pieces, 1, 128), F32),
            pltpu.VMEM((rounds, 1, 128), F32),
            pltpu.VMEM((rounds, 4, 1, 128), F32),
            dma((pieces, blocks)),
            dma((pieces, blocks)),
            dma((pieces, blocks)),
            dma((pieces, blocks)),
            dma((others, blocks)),
            dma((others, blocks)),
            dma((others, blocks)),
            dma((2, blocks)),
            dma((2, blocks)),
            dma((others, blocks)),
            dma((others, blocks)),
            dma((3,)),
            dma((3,)),
            dma((2,)),
            dma((2,)),
            dma((rounds,)),
            dma((rounds,)),
            dma((4,)),
        ],
        compiler_params=pltpu.CompilerParams(
            collective_id=0, has_side_effects=True, vmem_limit_bytes=48 * 1024 * 1024
        ),
    )(*operands)
    return write(proj, last, env)


def solution(mesh):
    placed = (
        P("sector", None, None),
        P("term", "sector", None, None),
        P("term", "sector", None, None),
        P("term", "sector"),
        P(None, "sector"),
        P("sector", None, None),
    )
    return jax.shard_map(
        on_device,
        mesh=mesh,
        in_specs=placed,
        out_specs=(P(), P("sector", "term", None), P("term", "sector", None, None)),
        check_vma=False,
    )
```

```python
import functools
import jax
import jax.numpy as jnp
from jax import lax
from jax.experimental import pallas as pl
from jax.experimental.pallas import tpu as pltpu
from jax.sharding import PartitionSpec as P

epsilon = 1e-06
MESH = pl.DeviceIdType.MESH
F32 = jnp.float32
BF16 = jnp.bfloat16


def fold(values):
    rows, width = values.shape
    total = values.reshape(rows // 8, 8, width).sum(axis=0)
    out = total[:, :128]
    for start in range(128, width, 128):
        out = out + total[:, start : start + 128]
    return out


def rounds_of(devices):
    out, stride = [], 1
    while stride < devices:
        radix = 4 if devices // stride % 4 == 0 else 2
        out.append((stride, radix))
        stride *= radix
    return out


def kernel(
    sizes, relays, early,
    dims, conn, psi_in, left_in, right_in, pre_in,
    proj, last, env,
    left, right, pre, psi, inverse_of, raw, far1, far2, far3, ext1, ext2, ext3, acc, stage, came, mine, given, other2, sig1, sig2, base1, base2,
    pre_far, sig_out, sig_far, base_far, tile, slots, norm_tile, norm_slots,
    on_send, on_recv, off_send, off_recv, relay_send, share_send, share_recv, mine_send, mine_recv, part_send, part_recv,
    pre_send, pre_recv, sig_send, sig_recv, sum_send, sum_recv, norm_send, norm_recv, load,
):
    pieces, devices, terms, blocks, width, entries = sizes
    share = width // pieces
    count = pieces * devices
    step = min(32, share)
    steps = share // step
    me_t = lax.axis_index("term")
    me_s = lax.axis_index("sector")
    me = me_t * devices + me_s
    first = me_s * blocks - blocks
    paired = pieces == 2
    odd = lax.rem(me_s, 2)
    on_s = me_s + 1 - 2 * odd
    off_s = me_s - 1 + 2 * odd
    has_off = (off_s >= 0) & (off_s < devices)
    zero = jnp.zeros((8, 128), F32)
    rounds = rounds_of(devices)

    def order(k):
        return k + odd * (blocks - 1 - 2 * k)

    def turn(k):
        return blocks - 1 - k + odd * (2 * k - blocks + 1)

    def device_at(offset):
        other = lax.rem(me + offset, count)
        return (other // devices, lax.rem(other, devices))

    def term_at(offset):
        return lax.rem(me_t + offset, pieces)

    def rows_of(piece):
        return pl.ds(pl.multiple_of(piece * share, share), share)

    def part_rows(j):
        return rows_of(term_at(pieces - j))

    everything = pl.ds(0, width)

    def arrived(view, sem):
        pltpu.make_async_copy(view, view, sem).wait()

    loads = [
        pltpu.make_async_copy(source, target, load.at[i])
        for i, (source, target) in enumerate(
            ((psi_in, psi), (pre_in, pre), (left_in, left), (right_in, right))
        )
    ]
    loads[0].start()

    barrier = pltpu.get_barrier_semaphore()

    def greet(t, s):
        pl.semaphore_signal(barrier, inc=1, device_id=(t, s), device_id_type=MESH)

    def peers(stride, radix):
        digit = lax.rem(me_s // stride, radix)
        return digit, [
            me_s + (lax.rem(digit + d, radix) - digit) * stride for d in range(1, radix)
        ]

    greeted = pieces - 1
    for stride, radix in rounds:
        for other in peers(stride, radix)[1]:
            greet(me_t, other)
        greeted += radix - 1
    for j in range(1, pieces):
        greet(term_at(j), me_s)
    apart = has_off & (off_s // rounds[0][1] != me_s // rounds[0][1])

    @pl.when(apart)
    def _():
        greet(me_t, off_s)

    loads[0].wait()
    for one in loads[1:]:
        one.start()


    def on_copy(ref, s, j, rows):
        return pltpu.make_async_remote_copy(
            src_ref=ref.at[blocks + s, rows],
            dst_ref=ref.at[s + odd * 2 * blocks, rows],
            send_sem=on_send.at[j, s],
            recv_sem=on_recv.at[j, s],
            device_id=(me_t, on_s),
            device_id_type=MESH,
        )

    def on_arrived(ref, s, j, rows):
        arrived(ref.at[s + (1 - odd) * 2 * blocks, rows], on_recv.at[j, s])

    def off_copy(ref, far, s, j):
        return pltpu.make_async_remote_copy(
            src_ref=ref.at[blocks + s, part_rows(j)],
            dst_ref=far.at[s, part_rows(j)],
            send_sem=off_send.at[j, s],
            recv_sem=off_recv.at[j, s],
            device_id=(me_t, off_s),
            device_id_type=MESH,
        )

    def off_slot(s):
        return s + odd * 2 * blocks

    def off_arrived(far, s, j):
        arrived(far.at[s, part_rows(j)], off_recv.at[j, s])

    def pre_copy(k):
        return pltpu.make_async_remote_copy(
            src_ref=pre.at[order(k)],
            dst_ref=pre_far.at[k],
            send_sem=pre_send.at[k],
            recv_sem=pre_recv.at[k],
            device_id=(me_t, off_s),
            device_id_type=MESH,
        )

    def sig_copy(which, k, j):
        return pltpu.make_async_remote_copy(
            src_ref=sig_out.at[which, k, part_rows(j)],
            dst_ref=sig_far.at[which, k, part_rows(j)],
            send_sem=sig_send.at[which, j, k],
            recv_sem=sig_recv.at[which, j, k],
            device_id=(me_t, off_s),
            device_id_type=MESH,
        )

    def relay_copy(far, s, j):
        return pltpu.make_async_remote_copy(
            src_ref=far.at[s, rows_of(me_t)],
            dst_ref=far.at[s, rows_of(me_t)],
            send_sem=relay_send.at[j - 1, s],
            recv_sem=off_recv.at[j, s],
            device_id=(term_at(j), me_s),
            device_id_type=MESH,
        )

    def relayed(k, span):
        return (k >= span[0]) & (k < span[1])

    def relay(far, k, span):
        @pl.when(has_off & relayed(k, span))
        def _():
            s = turn(k)
            off_arrived(far, s, 0)
            for j in range(1, pieces):
                relay_copy(far, s, j).start()

    def receive(far, k, span, low):
        s = turn(k)

        @pl.when(has_off & (k >= low) & jnp.logical_not(relayed(k, span)))
        def _():
            off_arrived(far, s, 0)

        @pl.when(has_off & (k >= low))
        def _():
            for j in range(1, pieces):
                off_arrived(far, s, j)

    def sent(ref, far, span, low, which):
        whole = which is None

        @pl.loop(0, blocks)
        def _(k):
            s = order(k)
            if whole:
                on_copy(ref, s, 0, everything).wait_send()
            else:
                for j in range(pieces):
                    on_copy(ref, s, j, part_rows(j)).wait_send()
                if not paired:
                    for offset in range(1, pieces):
                        share_copy(ref, s, offset, me_t).wait_send()

            @pl.when(has_off & (k >= low))
            def _():
                off_copy(ref, far, s, 0).wait_send()

            @pl.when(has_off & (k >= low) & jnp.logical_not(relayed(k, span)))
            def _():
                for j in range(1, pieces):
                    off_copy(ref, far, s, j).wait_send()

            @pl.when(has_off & relayed(k, span))
            def _():
                for j in range(1, pieces):
                    relay_copy(far, turn(k), j).wait_send()

        @pl.when(has_off)
        def _():
            for k in range(early):
                if whole:
                    pre_copy(k).wait_send()
                else:
                    for j in range(pieces):
                        sig_copy(which, k, j).wait_send()

    def share_copy(ref, s, offset, piece):
        return pltpu.make_async_remote_copy(
            src_ref=ref.at[blocks + s, rows_of(piece)],
            dst_ref=ref.at[blocks + s, rows_of(piece)],
            send_sem=share_send.at[offset - 1, s],
            recv_sem=share_recv.at[offset - 1, s],
            device_id=(term_at(offset), me_s),
            device_id_type=MESH,
        )

    def mine_copy(which, s):
        return pltpu.make_async_remote_copy(
            src_ref=mine.at[s],
            dst_ref=given.at[which, s],
            send_sem=mine_send.at[which, s],
            recv_sem=mine_recv.at[which, s],
            device_id=(term_at(1), me_s),
            device_id_type=MESH,
        )

    def part_copy(s, offset):
        return pltpu.make_async_remote_copy(
            src_ref=stage.at[offset - 1, s],
            dst_ref=came.at[offset - 1, s],
            send_sem=part_send.at[offset - 1, s],
            recv_sem=part_recv.at[offset - 1, s],
            device_id=(term_at(offset), me_s),
            device_id_type=MESH,
        )

    lane = lax.broadcasted_iota(jnp.int32, (1, 128), 1)

    def pack(tiles):
        packed = jnp.zeros((1, 128), F32)
        for i, one in enumerate(tiles):
            row = jnp.sum(one, axis=0, keepdims=True)
            packed = jnp.where(lane == i, jnp.sum(row, axis=1, keepdims=True), packed)
        return packed

    def sum_start(which, tiles):
        packed = pack(tiles)
        tile[which] = packed
        slots[which, me] = packed

        @pl.loop(1, count)
        def _(offset):
            pltpu.make_async_remote_copy(
                src_ref=tile.at[which],
                dst_ref=slots.at[which, me],
                send_sem=sum_send.at[which],
                recv_sem=sum_recv.at[which],
                device_id=device_at(offset),
                device_id_type=MESH,
            ).start()

    def sum_finish(which):
        others = slots.at[which, pl.ds(0, count - 1)]
        arrived(others, sum_recv.at[which])
        full = jnp.sum(slots[which], axis=0) / entries
        return lambda i: full[:, i : i + 1]

    def norm_start(i, packed):
        digit, others = peers(*rounds[i])
        norm_tile[i] = packed
        norm_slots[i, digit] = packed
        for other in others:
            pltpu.make_async_remote_copy(
                src_ref=norm_tile.at[i],
                dst_ref=norm_slots.at[i, digit],
                send_sem=norm_send.at[i],
                recv_sem=norm_recv.at[i],
                device_id=(me_t, other),
                device_id_type=MESH,
            ).start()

    def norm_finish(i):
        radix = rounds[i][1]
        arrived(norm_slots.at[i, pl.ds(0, radix - 1)], norm_recv.at[i])
        return jnp.sum(norm_slots[i, pl.ds(0, radix)], axis=0)

    starts = [k * step for k in range(steps)]
    strips = list(range(0, width, step))

    def own_rows(start):
        return pl.ds(pl.multiple_of(me_t * share + start, step), step)

    span0 = relays[0]

    def first_step(k, total):
        s = order(k)
        for start in strips:
            here = pl.ds(start, step)
            rows = lax.broadcasted_iota(jnp.int32, (step, width), 0) + start
            cols = lax.broadcasted_iota(jnp.int32, (step, width), 1)
            keep = (rows < dims[0, s]) & (cols < dims[1, s])
            v = jnp.where(keep, psi[s, here, :].astype(F32), 0.0)
            raw[blocks + s, here, :] = v.astype(BF16)
            total = total + fold(v * v)
        return total

    own_norm = pack([lax.fori_loop(0, blocks, first_step, zero)])
    pl.semaphore_wait(barrier, greeted + apart.astype(jnp.int32))
    norm_start(0, own_norm)

    @pl.loop(0, blocks)
    def _(k):
        s = order(k)
        on_copy(raw, s, 0, everything).start()

        @pl.when(has_off)
        def _():
            off_copy(raw, far1, s, 0).start()

        @pl.when(has_off & jnp.logical_not(relayed(k, span0)))
        def _():
            for j in range(1, pieces):
                off_copy(raw, far1, s, j).start()

    loads[1].wait()

    @pl.loop(0, blocks)
    def _(s):
        for start in strips:
            here = pl.ds(start, step)
            inverse_of[s, here, :] = 1.0 / pre[s, here, :].astype(F32)

    @pl.when(has_off)
    def _():
        for k in range(early):
            pre_copy(k).start()

    total = None
    for i in range(len(rounds)):
        total = norm_finish(i)
        if i + 1 < len(rounds):
            norm_start(i + 1, total)
        if i == 0:
            for k in range(relays[0][2]):
                relay(far1, k, span0)
    norm = total[:, 0:1] / entries
    scale = 1.0 / jnp.sqrt(norm + epsilon)

    def scaled(source, place, slot):
        for start in strips:
            here = pl.ds(start, step)
            ext1[slot, here, :] = (source[place, here, :].astype(F32) * scale).astype(BF16)

    @pl.loop(0, blocks)
    def _(s):
        scaled(raw, blocks + s, blocks + s)
        for start in starts:
            base1[s, pl.ds(start, step), :] = raw[blocks + s, own_rows(start), :].astype(F32) * scale

    @pl.loop(0, blocks)
    def _(k):
        s = turn(k)
        on_arrived(raw, s, 0, everything)
        slot = s + (1 - odd) * 2 * blocks
        scaled(raw, slot, slot)

    def product(ref, s, keep):
        halves = []
        for t in range(terms):
            source = ref[jnp.clip(conn[t, s] - first, 0, 3 * blocks - 1)]
            one = jnp.dot(left[t, s], source, preferred_element_type=F32).astype(BF16)
            halves.append(one)
            if keep:
                env[t, s] = one
        total = None
        for t in range(terms):
            one = lax.dot_general(
                halves[t], right[t, s], (((1,), (1,)), ((), ())), preferred_element_type=F32
            )
            total = one if total is None else total + one
        return total

    def take(ref, far, k, span, which, far_of):
        s = turn(k)
        low = 0 if which is None else early
        relay(far, k + span[2], span)
        receive(far, k, span, low)

        @pl.when(has_off & (k >= low))
        def _():
            if which is None:
                scaled(far, s, off_slot(s))
            else:
                ref[off_slot(s)] = far[s]

        if low:

            @pl.when(has_off & (k < low))
            def _():
                if which == 0:
                    arrived(pre_far.at[k], pre_recv.at[k])
                for j in range(pieces):
                    arrived(sig_far.at[which, k, part_rows(j)], sig_recv.at[which, j, k])
                for start in strips:
                    here = pl.ds(start, step)
                    b1 = far1[s, here, :].astype(F32) * scale
                    sigma = sig_far[which, k, here, :].astype(F32)
                    inverse = 1.0 / pre_far[k, here, :].astype(F32)
                    ref[off_slot(s), here, :] = far_of(k, here, sigma, b1, inverse).astype(BF16)

    def apply(ref, far, span, which, far_of):
        @pl.loop(0, blocks)
        def _(k):
            take(ref, far, k, span, which, far_of)
            s = turn(k)
            acc[s] = product(ref, s, False)
            for offset in range(1, pieces):
                stage[offset - 1, s] = acc[s, rows_of(term_at(offset)), :].astype(BF16)
                part_copy(s, offset).start()

    def masked(s, base, total):
        rows = lax.broadcasted_iota(jnp.int32, (step, width), 0) + base
        cols = lax.broadcasted_iota(jnp.int32, (step, width), 1)
        return jnp.where((rows < dims[0, s]) & (cols < dims[1, s]), total, 0.0)

    def masked_sum(s, start):
        total = acc[s, own_rows(start), :]
        for offset in range(1, pieces):
            total = total + came[offset - 1, s, pl.ds(start, step), :].astype(F32)
        return masked(s, me_t * share + start, total)

    def other_rows(start):
        return pl.ds(pl.multiple_of(term_at(1) * share + start, step), step)

    def other_sum(which, s, start):
        total = acc[s, other_rows(start), :] + given[which, s, pl.ds(start, step), :].astype(F32)
        return masked(s, term_at(1) * share + start, total)

    def give(which):
        if not paired:
            return

        for k in range(early):
            s = order(k)
            for start in starts:
                sigma = (sig1, sig2)[which][s, pl.ds(start, step), :]
                sig_out[which, k, own_rows(start), :] = sigma.astype(BF16)

            @pl.when(has_off)
            def _():
                sig_copy(which, k, 0).start()

        @pl.loop(0, blocks)
        def _(k):
            s = order(k)
            mine[s] = acc[s, rows_of(me_t), :].astype(BF16)
            mine_copy(which, s).start()

        for k in range(early):
            s = order(k)
            mine_copy(which, s).wait()
            for start in starts:
                sigma = other_sum(which, s, start)
                sig_out[which, k, other_rows(start), :] = sigma.astype(BF16)

            @pl.when(has_off)
            def _():
                sig_copy(which, k, 1).start()

    def divided(s, start):
        return inverse_of[s, own_rows(start), :]

    def part_wait(s):
        for offset in range(1, pieces):
            part_copy(s, offset).wait()

    def spread(which, ref, far, out, corr_of, other_of, span):
        @pl.loop(0, blocks)
        def _(k):
            s = order(k)
            for start in starts:
                value = corr_of(s, start)
                out[s, pl.ds(start, step), :] = value
                ref[blocks + s, own_rows(start), :] = value.astype(BF16)

            if not paired:
                for offset in range(1, pieces):
                    share_copy(ref, s, offset, me_t).start()
            on_copy(ref, s, 0, part_rows(0)).start()

            @pl.when(has_off & (k >= early))
            def _():
                off_copy(ref, far, s, 0).start()

            if paired:
                finish_block(which, ref, far, other_of, span, k)

        if not paired:

            @pl.loop(0, blocks)
            def _(k):
                finish_block(which, ref, far, other_of, span, k)

        for k in range(span[2]):
            relay(far, k, span)

    def finish_block(which, ref, far, other_of, span, k):
        s = order(k)
        if paired:
            @pl.when(k >= early)
            def _():
                mine_copy(which, s).wait()

            for start in starts:
                value = other_of(s, start, other_sum(which, s, start))
                ref[blocks + s, other_rows(start), :] = value.astype(BF16)
        for offset in range(1, pieces):
            if not paired:
                arrived(ref.at[blocks + s, part_rows(offset)], share_recv.at[offset - 1, s])
            on_copy(ref, s, offset, part_rows(offset)).start()

            @pl.when(has_off & (k >= early) & jnp.logical_not(relayed(k, span)))
            def _():
                off_copy(ref, far, s, offset).start()

    def settle(ref):
        @pl.loop(0, blocks)
        def _(k):
            s = turn(k)
            for j in range(pieces):
                on_arrived(ref, s, j, part_rows(j))

    loads[2].wait()
    loads[3].wait()
    apply(ext1, far1, span0, None, None)

    def sums1(k, totals):
        s = turn(k)
        part_wait(s)
        for start in starts:
            totals = sums1_rows(s, start, totals)
        return totals

    def sums1_rows(s, start, totals):
        here = pl.ds(start, step)
        sigma = masked_sum(s, start)
        sig1[s, here, :] = sigma
        inverse = divided(s, start)
        b1 = base1[s, here, :]
        r = sigma * inverse
        q = b1 * inverse
        pairs = [(b1, sigma), (b1, r), (b1, q), (r, r), (r, q), (q, q), (b1, b1)]
        return tuple(t + fold(x * y) for t, (x, y) in zip(totals, pairs))

    sum_start(0, lax.fori_loop(0, blocks, sums1, (zero,) * 7))
    give(0)
    sent(raw, far1, span0, 0, None)
    got = sum_finish(0)
    theta1 = got(0)
    first_gram = got(6)
    weight = got(1) - theta1 * got(2)
    length = (
        (got(3) - 2.0 * theta1 * got(4) + theta1 * theta1 * got(5))
        - 2.0 * weight * weight
        + weight * weight * first_gram
    )
    scale1 = 1.0 / jnp.sqrt(jnp.maximum(length, 0.0) + epsilon)

    def corr1(s, start):
        here = pl.ds(start, step)
        b1 = base1[s, here, :]
        corr = (sig1[s, here, :] - theta1 * b1) * divided(s, start)
        return (corr - weight * b1) * scale1

    def first_other(s, start):
        return raw[blocks + s, other_rows(start), :].astype(F32) * scale

    def other1(s, start, sigma):
        b1 = first_other(s, start)
        corr = (sigma - theta1 * b1) * inverse_of[s, other_rows(start), :]
        value = (corr - weight * b1) * scale1
        other2[s, pl.ds(start, step), :] = value
        return value

    spread(0, ext2, far2, base2, corr1, other1, relays[1])
    settle(ext2)
    def far1_of(k, here, sigma, b1, inverse):
        value = ((sigma - theta1 * b1) * inverse - weight * b1) * scale1
        base_far[k, here, :] = value
        return value

    def far2_of(k, here, sigma, b1, inverse):
        b2 = base_far[k, here, :]
        return ((sigma - theta2 * b2) * inverse - weight1 * b1 - weight2 * b2) * scale2

    apply(ext2, far2, relays[1], 0, far1_of)

    def sums2(k, totals):
        s = turn(k)
        part_wait(s)
        for start in starts:
            totals = sums2_rows(s, start, totals)
        return totals

    def sums2_rows(s, start, totals):
        here = pl.ds(start, step)
        sigma = masked_sum(s, start)
        sig2[s, here, :] = sigma
        inverse = divided(s, start)
        b1 = base1[s, here, :]
        b2 = base2[s, here, :]
        r = sigma * inverse
        q = b2 * inverse
        pairs = [
            (b2, sigma), (b1, r), (b2, r), (b1, q), (b2, q), (r, r), (r, q), (q, q),
            (b1, b2), (b2, b2), (b1, sigma), (b2, sig1[s, here, :]),
        ]
        return tuple(t + fold(x * y) for t, (x, y) in zip(totals, pairs))

    sum_start(1, lax.fori_loop(0, blocks, sums2, (zero,) * 12))
    give(1)
    sent(ext2, far2, relays[1], early, 0)
    more = sum_finish(1)
    theta2 = more(0)
    weight1 = more(1) - theta2 * more(3)
    weight2 = more(2) - theta2 * more(4)
    length2 = (
        (more(5) - 2.0 * theta2 * more(6) + theta2 * theta2 * more(7))
        - 2.0 * (weight1 * weight1 + weight2 * weight2)
        + weight1 * weight1 * first_gram
        + 2.0 * weight1 * weight2 * more(8)
        + weight2 * weight2 * more(9)
    )
    scale2 = 1.0 / jnp.sqrt(jnp.maximum(length2, 0.0) + epsilon)

    def corr2(s, start):
        here = pl.ds(start, step)
        b1 = base1[s, here, :]
        b2 = base2[s, here, :]
        corr = (sig2[s, here, :] - theta2 * b2) * divided(s, start)
        return (corr - weight1 * b1 - weight2 * b2) * scale2

    def other2_of(s, start, sigma):
        b1 = first_other(s, start)
        b2 = other2[s, pl.ds(start, step), :]
        corr = (sigma - theta2 * b2) * inverse_of[s, other_rows(start), :]
        return (corr - weight1 * b1 - weight2 * b2) * scale2

    def cross(s, totals):
        for start in starts:
            here = pl.ds(start, step)
            b3 = last[s, here, :]
            pairs = [(b3, sig1[s, here, :]), (b3, sig2[s, here, :])]
            totals = tuple(t + fold(x * y) for t, (x, y) in zip(totals, pairs))
        return totals

    spread(1, ext3, far3, last, corr2, other2_of, relays[2])
    crossed = lax.fori_loop(0, blocks, cross, (zero,) * 2)
    settle(ext3)

    def sums3(k, totals):
        take(ext3, far3, k, relays[2], 1, far2_of)
        s = turn(k)
        acc[s] = product(ext3, s, True)

        for start in strips:
            here = pl.ds(start, step)
            sigma = acc[s, here, :]
            vectors = [ref[blocks + s, here, :].astype(F32) for ref in (ext1, ext2, ext3)]
            totals = tuple(t + fold(v * sigma) for t, v in zip(totals, vectors))
        return totals

    sum_start(2, list(lax.fori_loop(0, blocks, sums3, (zero,) * 3)) + list(crossed))

    @pl.loop(0, blocks)
    def _(s):
        own = ext3[blocks + s]
        for t in range(terms):
            new = lax.dot_general(
                own, env[t, s], (((0,), (0,)), ((), ())), preferred_element_type=F32
            )
            env[t, s] = (new * width ** (-0.5)).astype(BF16)

    sent(ext3, far3, relays[2], early, 1)
    end = sum_finish(2)
    cells = [
        [theta1, more(10), end(0)],
        [more(11), theta2, end(1)],
        [end(3), end(4), end(2)],
    ]
    row = lax.broadcasted_iota(jnp.int32, (8, 128), 0)
    col = lax.broadcasted_iota(jnp.int32, (8, 128), 1)
    out = zero
    for i in range(3):
        for j in range(3):
            out = jnp.where((row == i) & (col == j), cells[i][j], out)
    proj[...] = out

    for which in range(3):
        arrived(slots.at[which, pl.ds(0, count - 1)], sum_send.at[which])
    for i, (stride, radix) in enumerate(rounds):
        arrived(norm_slots.at[i, pl.ds(0, radix - 1)], norm_send.at[i])


def write_kernel(proj, last, env, proj_out, last_out, env_out, sem):
    copies = [
        pltpu.make_async_copy(last, last_out, sem.at[0]),
        pltpu.make_async_copy(env, env_out, sem.at[1]),
    ]
    for one in copies:
        one.start()
    proj_out[...] = proj[:3, :3]
    for one in copies:
        one.wait()


def write(proj, last, env):
    vmem = pl.BlockSpec(memory_space=pltpu.VMEM)
    anywhere = pl.BlockSpec(memory_space=pl.ANY)
    hbm = pl.BlockSpec(memory_space=pltpu.HBM)
    return pl.pallas_call(
        write_kernel,
        name="write",
        out_shape=(
            jax.ShapeDtypeStruct((3, 3), F32),
            jax.ShapeDtypeStruct(last.shape, F32),
            jax.ShapeDtypeStruct(env.shape, BF16),
        ),
        in_specs=[vmem, anywhere, anywhere],
        out_specs=(vmem, hbm, hbm),
        scratch_shapes=[pltpu.SemaphoreType.DMA((2,))],
        compiler_params=pltpu.CompilerParams(vmem_limit_bytes=12 * 1024 * 1024),
    )(proj, last, env)


EARLY = 2
RELAYS = ((0, 4, 4), (0, 0, 0), (2, 6, 5))


def on_device(psi, left, right, connect, sector_dims, precond):
    blocks, width = psi.shape[0], psi.shape[1]
    terms = left.shape[0]
    pieces, devices = lax.axis_size("term"), lax.axis_size("sector")
    count = pieces * devices
    share = width // pieces
    entries = float(blocks * devices * width * width)
    sizes = (pieces, devices, terms, blocks, width, entries)
    others = max(pieces - 1, 1)
    rounds = len(rounds_of(devices))
    early = min(EARLY, blocks) if pieces == 2 else 0
    ahead = max(early, 1)
    dma = pltpu.SemaphoreType.DMA
    vmem = pl.BlockSpec(memory_space=pltpu.VMEM)
    smem = pl.BlockSpec(memory_space=pltpu.SMEM)
    hbm = pl.BlockSpec(memory_space=pltpu.HBM)
    operands = [
        pltpu.with_memory_space_constraint(one, pltpu.HBM)
        for one in (sector_dims, connect, psi, left, right, precond)
    ]
    proj, last, env = pl.pallas_call(
        functools.partial(kernel, sizes, RELAYS, early),
        name="davidson",
        out_shape=(
            jax.ShapeDtypeStruct((8, 128), F32),
            pltpu.VMEM((blocks, share, width), F32),
            pltpu.VMEM((terms, blocks, width, width), BF16),
        ),
        in_specs=[smem, smem, hbm, hbm, hbm, hbm],
        out_specs=(vmem, vmem, vmem),
        scratch_shapes=[
            pltpu.VMEM((terms, blocks, width, width), BF16),
            pltpu.VMEM((terms, blocks, width, width), BF16),
            pltpu.VMEM((blocks, width, width), BF16),
            pltpu.VMEM((blocks, width, width), BF16),
            pltpu.VMEM((blocks, width, width), F32),
            pltpu.VMEM((3 * blocks, width, width), BF16),
            pltpu.VMEM((blocks, width, width), BF16),
            pltpu.VMEM((blocks, width, width), BF16),
            pltpu.VMEM((blocks, width, width), BF16),
            pltpu.VMEM((3 * blocks, width, width), BF16),
            pltpu.VMEM((3 * blocks, width, width), BF16),
            pltpu.VMEM((3 * blocks, width, width), BF16),
            pltpu.VMEM((blocks, width, width), F32),
            pltpu.VMEM((others, blocks, share, width), BF16),
            pltpu.VMEM((others, blocks, share, width), BF16),
            pltpu.VMEM((blocks, share, width), BF16),
            pltpu.VMEM((2, blocks, share, width), BF16),
            pltpu.VMEM((blocks, share, width), F32),
            pltpu.VMEM((blocks, share, width), F32),
            pltpu.VMEM((blocks, share, width), F32),
            pltpu.VMEM((blocks, share, width), F32),
            pltpu.VMEM((blocks, share, width), F32),
            pltpu.VMEM((ahead, width, width), BF16),
            pltpu.VMEM((2, ahead, width, width), BF16),
            pltpu.VMEM((2, ahead, width, width), BF16),
            pltpu.VMEM((ahead, width, width), F32),
            pltpu.VMEM((3, 1, 128), F32),
            pltpu.VMEM((3, count, 1, 128), F32),
            pltpu.VMEM((rounds, 1, 128), F32),
            pltpu.VMEM((rounds, 4, 1, 128), F32),
            dma((pieces, blocks)),
            dma((pieces, blocks)),
            dma((pieces, blocks)),
            dma((pieces, blocks)),
            dma((others, blocks)),
            dma((others, blocks)),
            dma((others, blocks)),
            dma((2, blocks)),
            dma((2, blocks)),
            dma((others, blocks)),
            dma((others, blocks)),
            dma((ahead,)),
            dma((ahead,)),
            dma((2, pieces, ahead)),
            dma((2, pieces, ahead)),
            dma((3,)),
            dma((3,)),
            dma((rounds,)),
            dma((rounds,)),
            dma((4,)),
        ],
        compiler_params=pltpu.CompilerParams(
            collective_id=0, has_side_effects=True, vmem_limit_bytes=48 * 1024 * 1024
        ),
    )(*operands)
    return write(proj, last, env)


def solution(mesh):
    placed = (
        P("sector", None, None),
        P("term", "sector", None, None),
        P("term", "sector", None, None),
        P("term", "sector"),
        P(None, "sector"),
        P("sector", None, None),
    )
    return jax.shard_map(
        on_device,
        mesh=mesh,
        in_specs=placed,
        out_specs=(P(), P("sector", "term", None), P("term", "sector", None, None)),
        check_vma=False,
    )
```

```python
import functools
import jax
import jax.numpy as jnp
from jax import lax
from jax.experimental import pallas as pl
from jax.experimental.pallas import tpu as pltpu
from jax.sharding import PartitionSpec as P

epsilon = 1e-06
MESH = pl.DeviceIdType.MESH
F32 = jnp.float32
BF16 = jnp.bfloat16


def fold(values):
    rows, width = values.shape
    total = values.reshape(rows // 8, 8, width).sum(axis=0)
    out = total[:, :128]
    for start in range(128, width, 128):
        out = out + total[:, start : start + 128]
    return out


def rounds_of(devices):
    out, stride = [], 1
    while stride < devices:
        radix = 4 if devices // stride % 4 == 0 else 2
        out.append((stride, radix))
        stride *= radix
    return out


def kernel(
    sizes, relays, early,
    dims, conn, psi_in, left_in, right_in, pre_in,
    proj, last, env,
    left, right, pre, psi, inverse_of, raw, far1, far2, far3, ext1, ext2, ext3, acc, stage, came, mine, given, other2, sig1, sig2, base1, base2,
    pre_far, sig_out, sig_far, base_far, tile, slots, norm_tile, norm_slots,
    on_send, on_recv, off_send, off_recv, relay_send, share_send, share_recv, mine_send, mine_recv, part_send, part_recv,
    pre_send, pre_recv, sig_send, sig_recv, sum_send, sum_recv, norm_send, norm_recv, load,
):
    pieces, devices, terms, blocks, width, entries = sizes
    share = width // pieces
    count = pieces * devices
    step = min(32, share)
    steps = share // step
    me_t = lax.axis_index("term")
    me_s = lax.axis_index("sector")
    me = me_t * devices + me_s
    first = me_s * blocks - blocks
    paired = pieces == 2
    odd = lax.rem(me_s, 2)
    on_s = me_s + 1 - 2 * odd
    off_s = me_s - 1 + 2 * odd
    has_off = (off_s >= 0) & (off_s < devices)
    zero = jnp.zeros((8, 128), F32)
    rounds = rounds_of(devices)

    def order(k):
        return k + odd * (blocks - 1 - 2 * k)

    def turn(k):
        return blocks - 1 - k + odd * (2 * k - blocks + 1)

    def device_at(offset):
        other = lax.rem(me + offset, count)
        return (other // devices, lax.rem(other, devices))

    def term_at(offset):
        return lax.rem(me_t + offset, pieces)

    def rows_of(piece):
        return pl.ds(pl.multiple_of(piece * share, share), share)

    def part_rows(j):
        return rows_of(term_at(pieces - j))

    everything = pl.ds(0, width)

    def arrived(view, sem):
        pltpu.make_async_copy(view, view, sem).wait()

    loads = [
        pltpu.make_async_copy(source, target, load.at[i])
        for i, (source, target) in enumerate(
            ((psi_in, psi), (pre_in, pre), (left_in, left), (right_in, right))
        )
    ]
    loads[0].start()

    barrier = pltpu.get_barrier_semaphore()

    def greet(t, s):
        pl.semaphore_signal(barrier, inc=1, device_id=(t, s), device_id_type=MESH)

    def peers(stride, radix):
        digit = lax.rem(me_s // stride, radix)
        return digit, [
            me_s + (lax.rem(digit + d, radix) - digit) * stride for d in range(1, radix)
        ]

    greeted = pieces - 1
    for stride, radix in rounds:
        for other in peers(stride, radix)[1]:
            greet(me_t, other)
        greeted += radix - 1
    for j in range(1, pieces):
        greet(term_at(j), me_s)
    apart = has_off & (off_s // rounds[0][1] != me_s // rounds[0][1])

    @pl.when(apart)
    def _():
        greet(me_t, off_s)

    loads[0].wait()
    for one in loads[1:]:
        one.start()


    def on_copy(ref, s, j, rows):
        return pltpu.make_async_remote_copy(
            src_ref=ref.at[blocks + s, rows],
            dst_ref=ref.at[s + odd * 2 * blocks, rows],
            send_sem=on_send.at[j, s],
            recv_sem=on_recv.at[j, s],
            device_id=(me_t, on_s),
            device_id_type=MESH,
        )

    def on_arrived(ref, s, j, rows):
        arrived(ref.at[s + (1 - odd) * 2 * blocks, rows], on_recv.at[j, s])

    def off_copy(ref, far, s, j):
        return pltpu.make_async_remote_copy(
            src_ref=ref.at[blocks + s, part_rows(j)],
            dst_ref=far.at[s, part_rows(j)],
            send_sem=off_send.at[j, s],
            recv_sem=off_recv.at[j, s],
            device_id=(me_t, off_s),
            device_id_type=MESH,
        )

    def off_slot(s):
        return s + odd * 2 * blocks

    def off_arrived(far, s, j):
        arrived(far.at[s, part_rows(j)], off_recv.at[j, s])

    def pre_copy(k):
        return pltpu.make_async_remote_copy(
            src_ref=pre.at[order(k)],
            dst_ref=pre_far.at[k],
            send_sem=pre_send.at[k],
            recv_sem=pre_recv.at[k],
            device_id=(me_t, off_s),
            device_id_type=MESH,
        )

    def sig_copy(which, k, j):
        return pltpu.make_async_remote_copy(
            src_ref=sig_out.at[which, k, part_rows(j)],
            dst_ref=sig_far.at[which, k, part_rows(j)],
            send_sem=sig_send.at[which, j, k],
            recv_sem=sig_recv.at[which, j, k],
            device_id=(me_t, off_s),
            device_id_type=MESH,
        )

    def relay_copy(far, s, j):
        return pltpu.make_async_remote_copy(
            src_ref=far.at[s, rows_of(me_t)],
            dst_ref=far.at[s, rows_of(me_t)],
            send_sem=relay_send.at[j - 1, s],
            recv_sem=off_recv.at[j, s],
            device_id=(term_at(j), me_s),
            device_id_type=MESH,
        )

    def relayed(k, span):
        return (k >= span[0]) & (k < span[1])

    def relay(far, k, span):
        @pl.when(has_off & relayed(k, span))
        def _():
            s = turn(k)
            off_arrived(far, s, 0)
            for j in range(1, pieces):
                relay_copy(far, s, j).start()

    def receive(far, k, span, low):
        s = turn(k)

        @pl.when(has_off & (k >= low) & jnp.logical_not(relayed(k, span)))
        def _():
            off_arrived(far, s, 0)

        @pl.when(has_off & (k >= low))
        def _():
            for j in range(1, pieces):
                off_arrived(far, s, j)

    def sent(ref, far, span, low, which):
        whole = which is None

        @pl.loop(0, blocks)
        def _(k):
            s = order(k)
            if whole:
                on_copy(ref, s, 0, everything).wait_send()
            else:
                for j in range(pieces):
                    on_copy(ref, s, j, part_rows(j)).wait_send()
                if not paired:
                    for offset in range(1, pieces):
                        share_copy(ref, s, offset, me_t).wait_send()

            @pl.when(has_off & (k >= low))
            def _():
                off_copy(ref, far, s, 0).wait_send()

            @pl.when(has_off & (k >= low) & jnp.logical_not(relayed(k, span)))
            def _():
                for j in range(1, pieces):
                    off_copy(ref, far, s, j).wait_send()

            @pl.when(has_off & relayed(k, span))
            def _():
                for j in range(1, pieces):
                    relay_copy(far, turn(k), j).wait_send()

        @pl.when(has_off)
        def _():
            for k in range(early):
                if whole:
                    pre_copy(k).wait_send()
                else:
                    for j in range(pieces):
                        sig_copy(which, k, j).wait_send()

    def share_copy(ref, s, offset, piece):
        return pltpu.make_async_remote_copy(
            src_ref=ref.at[blocks + s, rows_of(piece)],
            dst_ref=ref.at[blocks + s, rows_of(piece)],
            send_sem=share_send.at[offset - 1, s],
            recv_sem=share_recv.at[offset - 1, s],
            device_id=(term_at(offset), me_s),
            device_id_type=MESH,
        )

    def mine_copy(which, s):
        return pltpu.make_async_remote_copy(
            src_ref=mine.at[s],
            dst_ref=given.at[which, s],
            send_sem=mine_send.at[which, s],
            recv_sem=mine_recv.at[which, s],
            device_id=(term_at(1), me_s),
            device_id_type=MESH,
        )

    def part_copy(s, offset):
        return pltpu.make_async_remote_copy(
            src_ref=stage.at[offset - 1, s],
            dst_ref=came.at[offset - 1, s],
            send_sem=part_send.at[offset - 1, s],
            recv_sem=part_recv.at[offset - 1, s],
            device_id=(term_at(offset), me_s),
            device_id_type=MESH,
        )

    lane = lax.broadcasted_iota(jnp.int32, (1, 128), 1)

    def pack(tiles):
        packed = jnp.zeros((1, 128), F32)
        for i, one in enumerate(tiles):
            row = jnp.sum(one, axis=0, keepdims=True)
            packed = jnp.where(lane == i, jnp.sum(row, axis=1, keepdims=True), packed)
        return packed

    def sum_start(which, tiles):
        packed = pack(tiles)
        tile[which] = packed
        slots[which, me] = packed

        @pl.loop(1, count)
        def _(offset):
            pltpu.make_async_remote_copy(
                src_ref=tile.at[which],
                dst_ref=slots.at[which, me],
                send_sem=sum_send.at[which],
                recv_sem=sum_recv.at[which],
                device_id=device_at(offset),
                device_id_type=MESH,
            ).start()

    def sum_finish(which):
        others = slots.at[which, pl.ds(0, count - 1)]
        arrived(others, sum_recv.at[which])
        full = jnp.sum(slots[which], axis=0) / entries
        return lambda i: full[:, i : i + 1]

    def norm_start(i, packed):
        digit, others = peers(*rounds[i])
        norm_tile[i] = packed
        norm_slots[i, digit] = packed
        for other in others:
            pltpu.make_async_remote_copy(
                src_ref=norm_tile.at[i],
                dst_ref=norm_slots.at[i, digit],
                send_sem=norm_send.at[i],
                recv_sem=norm_recv.at[i],
                device_id=(me_t, other),
                device_id_type=MESH,
            ).start()

    def norm_finish(i):
        radix = rounds[i][1]
        arrived(norm_slots.at[i, pl.ds(0, radix - 1)], norm_recv.at[i])
        return jnp.sum(norm_slots[i, pl.ds(0, radix)], axis=0)

    starts = [k * step for k in range(steps)]
    strips = list(range(0, width, step))

    def own_rows(start):
        return pl.ds(pl.multiple_of(me_t * share + start, step), step)

    span0 = relays[0]

    def first_step(k, total):
        s = order(k)
        for start in strips:
            here = pl.ds(start, step)
            rows = lax.broadcasted_iota(jnp.int32, (step, width), 0) + start
            cols = lax.broadcasted_iota(jnp.int32, (step, width), 1)
            keep = (rows < dims[0, s]) & (cols < dims[1, s])
            v = jnp.where(keep, psi[s, here, :].astype(F32), 0.0)
            raw[blocks + s, here, :] = v.astype(BF16)
            total = total + fold(v * v)
        return total

    own_norm = pack([lax.fori_loop(0, blocks, first_step, zero)])
    pl.semaphore_wait(barrier, greeted + apart.astype(jnp.int32))
    norm_start(0, own_norm)

    def first_off(low, high):
        @pl.loop(low, high)
        def _(k):
            s = order(k)

            @pl.when(has_off)
            def _():
                off_copy(raw, far1, s, 0).start()

            @pl.when(has_off & jnp.logical_not(relayed(k, span0)))
            def _():
                for j in range(1, pieces):
                    off_copy(raw, far1, s, j).start()

    first_off(0, HEAD)

    @pl.loop(0, blocks)
    def _(k):
        on_copy(raw, order(k), 0, everything).start()

    def finish_loads():
        loads[1].wait()

        @pl.loop(0, blocks)
        def _(s):
            for start in strips:
                here = pl.ds(start, step)
                inverse_of[s, here, :] = 1.0 / pre[s, here, :].astype(F32)

        @pl.when(has_off)
        def _():
            for k in range(early):
                pre_copy(k).start()

    total = None
    for i in range(len(rounds)):
        total = norm_finish(i)
        if i + 1 < len(rounds):
            norm_start(i + 1, total)
        if i == max(len(rounds) - 2, 0):
            first_off(HEAD, blocks)
            finish_loads()
            for k in range(relays[0][2]):
                relay(far1, k, span0)
    norm = total[:, 0:1] / entries
    scale = 1.0 / jnp.sqrt(norm + epsilon)

    def scaled(source, place, slot):
        for start in strips:
            here = pl.ds(start, step)
            ext1[slot, here, :] = (source[place, here, :].astype(F32) * scale).astype(BF16)

    @pl.loop(0, blocks)
    def _(s):
        scaled(raw, blocks + s, blocks + s)
        for start in starts:
            base1[s, pl.ds(start, step), :] = raw[blocks + s, own_rows(start), :].astype(F32) * scale

    @pl.loop(0, blocks)
    def _(k):
        s = turn(k)
        on_arrived(raw, s, 0, everything)
        slot = s + (1 - odd) * 2 * blocks
        scaled(raw, slot, slot)

    def product(ref, s, keep):
        halves = []
        for t in range(terms):
            source = ref[jnp.clip(conn[t, s] - first, 0, 3 * blocks - 1)]
            one = jnp.dot(left[t, s], source, preferred_element_type=F32).astype(BF16)
            halves.append(one)
            if keep:
                env[t, s] = one
        total = None
        for t in range(terms):
            one = lax.dot_general(
                halves[t], right[t, s], (((1,), (1,)), ((), ())), preferred_element_type=F32
            )
            total = one if total is None else total + one
        return total

    def take(ref, far, k, span, which, far_of):
        s = turn(k)
        low = 0 if which is None else early
        relay(far, k + span[2], span)
        receive(far, k, span, low)

        @pl.when(has_off & (k >= low))
        def _():
            if which is None:
                scaled(far, s, off_slot(s))
            else:
                ref[off_slot(s)] = far[s]

        if low:

            @pl.when(has_off & (k < low))
            def _():
                if which == 0:
                    arrived(pre_far.at[k], pre_recv.at[k])
                for j in range(pieces):
                    arrived(sig_far.at[which, k, part_rows(j)], sig_recv.at[which, j, k])
                for start in strips:
                    here = pl.ds(start, step)
                    b1 = far1[s, here, :].astype(F32) * scale
                    sigma = sig_far[which, k, here, :].astype(F32)
                    inverse = 1.0 / pre_far[k, here, :].astype(F32)
                    ref[off_slot(s), here, :] = far_of(k, here, sigma, b1, inverse).astype(BF16)

    def apply(ref, far, span, which, far_of):
        @pl.loop(0, blocks)
        def _(k):
            take(ref, far, k, span, which, far_of)
            s = turn(k)
            acc[s] = product(ref, s, False)
            for offset in range(1, pieces):
                stage[offset - 1, s] = acc[s, rows_of(term_at(offset)), :].astype(BF16)
                part_copy(s, offset).start()

    def masked(s, base, total):
        rows = lax.broadcasted_iota(jnp.int32, (step, width), 0) + base
        cols = lax.broadcasted_iota(jnp.int32, (step, width), 1)
        return jnp.where((rows < dims[0, s]) & (cols < dims[1, s]), total, 0.0)

    def masked_sum(s, start):
        total = acc[s, own_rows(start), :]
        for offset in range(1, pieces):
            total = total + came[offset - 1, s, pl.ds(start, step), :].astype(F32)
        return masked(s, me_t * share + start, total)

    def other_rows(start):
        return pl.ds(pl.multiple_of(term_at(1) * share + start, step), step)

    def other_sum(which, s, start):
        total = acc[s, other_rows(start), :] + given[which, s, pl.ds(start, step), :].astype(F32)
        return masked(s, term_at(1) * share + start, total)

    def give(which):
        if not paired:
            return

        for k in range(early):
            s = order(k)
            for start in starts:
                sigma = (sig1, sig2)[which][s, pl.ds(start, step), :]
                sig_out[which, k, own_rows(start), :] = sigma.astype(BF16)

            @pl.when(has_off)
            def _():
                sig_copy(which, k, 0).start()

        @pl.loop(0, blocks)
        def _(k):
            s = order(k)
            mine[s] = acc[s, rows_of(me_t), :].astype(BF16)
            mine_copy(which, s).start()

        for k in range(early):
            s = order(k)
            mine_copy(which, s).wait()
            for start in starts:
                sigma = other_sum(which, s, start)
                sig_out[which, k, other_rows(start), :] = sigma.astype(BF16)

            @pl.when(has_off)
            def _():
                sig_copy(which, k, 1).start()

    def divided(s, start):
        return inverse_of[s, own_rows(start), :]

    def part_wait(s):
        for offset in range(1, pieces):
            part_copy(s, offset).wait()

    def spread(which, ref, far, out, corr_of, other_of, span):
        @pl.loop(0, blocks)
        def _(k):
            s = order(k)
            for start in starts:
                value = corr_of(s, start)
                out[s, pl.ds(start, step), :] = value
                ref[blocks + s, own_rows(start), :] = value.astype(BF16)

            if not paired:
                for offset in range(1, pieces):
                    share_copy(ref, s, offset, me_t).start()
            on_copy(ref, s, 0, part_rows(0)).start()

            @pl.when(has_off & (k >= early))
            def _():
                off_copy(ref, far, s, 0).start()

            if paired:
                finish_block(which, ref, far, other_of, span, k)

        if not paired:

            @pl.loop(0, blocks)
            def _(k):
                finish_block(which, ref, far, other_of, span, k)

        for k in range(span[2]):
            relay(far, k, span)

    def finish_block(which, ref, far, other_of, span, k):
        s = order(k)
        if paired:
            @pl.when(k >= early)
            def _():
                mine_copy(which, s).wait()

            for start in starts:
                value = other_of(s, start, other_sum(which, s, start))
                ref[blocks + s, other_rows(start), :] = value.astype(BF16)
        for offset in range(1, pieces):
            if not paired:
                arrived(ref.at[blocks + s, part_rows(offset)], share_recv.at[offset - 1, s])
            on_copy(ref, s, offset, part_rows(offset)).start()

            @pl.when(has_off & (k >= early) & jnp.logical_not(relayed(k, span)))
            def _():
                off_copy(ref, far, s, offset).start()

    def settle(ref):
        @pl.loop(0, blocks)
        def _(k):
            s = turn(k)
            for j in range(pieces):
                on_arrived(ref, s, j, part_rows(j))

    loads[2].wait()
    loads[3].wait()
    apply(ext1, far1, span0, None, None)

    def sums1(k, totals):
        s = turn(k)
        part_wait(s)
        for start in starts:
            totals = sums1_rows(s, start, totals)
        return totals

    def sums1_rows(s, start, totals):
        here = pl.ds(start, step)
        sigma = masked_sum(s, start)
        sig1[s, here, :] = sigma
        inverse = divided(s, start)
        b1 = base1[s, here, :]
        r = sigma * inverse
        q = b1 * inverse
        pairs = [(b1, sigma), (b1, r), (b1, q), (r, r), (r, q), (q, q), (b1, b1)]
        return tuple(t + fold(x * y) for t, (x, y) in zip(totals, pairs))

    sum_start(0, lax.fori_loop(0, blocks, sums1, (zero,) * 7))
    give(0)
    sent(raw, far1, span0, 0, None)
    got = sum_finish(0)
    theta1 = got(0)
    first_gram = got(6)
    weight = got(1) - theta1 * got(2)
    length = (
        (got(3) - 2.0 * theta1 * got(4) + theta1 * theta1 * got(5))
        - 2.0 * weight * weight
        + weight * weight * first_gram
    )
    scale1 = 1.0 / jnp.sqrt(jnp.maximum(length, 0.0) + epsilon)

    def corr1(s, start):
        here = pl.ds(start, step)
        b1 = base1[s, here, :]
        corr = (sig1[s, here, :] - theta1 * b1) * divided(s, start)
        return (corr - weight * b1) * scale1

    def first_other(s, start):
        return raw[blocks + s, other_rows(start), :].astype(F32) * scale

    def other1(s, start, sigma):
        b1 = first_other(s, start)
        corr = (sigma - theta1 * b1) * inverse_of[s, other_rows(start), :]
        value = (corr - weight * b1) * scale1
        other2[s, pl.ds(start, step), :] = value
        return value

    spread(0, ext2, far2, base2, corr1, other1, relays[1])
    settle(ext2)
    def far1_of(k, here, sigma, b1, inverse):
        value = ((sigma - theta1 * b1) * inverse - weight * b1) * scale1
        base_far[k, here, :] = value
        return value

    def far2_of(k, here, sigma, b1, inverse):
        b2 = base_far[k, here, :]
        return ((sigma - theta2 * b2) * inverse - weight1 * b1 - weight2 * b2) * scale2

    apply(ext2, far2, relays[1], 0, far1_of)

    def sums2(k, totals):
        s = turn(k)
        part_wait(s)
        for start in starts:
            totals = sums2_rows(s, start, totals)
        return totals

    def sums2_rows(s, start, totals):
        here = pl.ds(start, step)
        sigma = masked_sum(s, start)
        sig2[s, here, :] = sigma
        inverse = divided(s, start)
        b1 = base1[s, here, :]
        b2 = base2[s, here, :]
        r = sigma * inverse
        q = b2 * inverse
        pairs = [
            (b2, sigma), (b1, r), (b2, r), (b1, q), (b2, q), (r, r), (r, q), (q, q),
            (b1, b2), (b2, b2), (b1, sigma), (b2, sig1[s, here, :]),
        ]
        return tuple(t + fold(x * y) for t, (x, y) in zip(totals, pairs))

    sum_start(1, lax.fori_loop(0, blocks, sums2, (zero,) * 12))
    give(1)
    sent(ext2, far2, relays[1], early, 0)
    more = sum_finish(1)
    theta2 = more(0)
    weight1 = more(1) - theta2 * more(3)
    weight2 = more(2) - theta2 * more(4)
    length2 = (
        (more(5) - 2.0 * theta2 * more(6) + theta2 * theta2 * more(7))
        - 2.0 * (weight1 * weight1 + weight2 * weight2)
        + weight1 * weight1 * first_gram
        + 2.0 * weight1 * weight2 * more(8)
        + weight2 * weight2 * more(9)
    )
    scale2 = 1.0 / jnp.sqrt(jnp.maximum(length2, 0.0) + epsilon)

    def corr2(s, start):
        here = pl.ds(start, step)
        b1 = base1[s, here, :]
        b2 = base2[s, here, :]
        corr = (sig2[s, here, :] - theta2 * b2) * divided(s, start)
        return (corr - weight1 * b1 - weight2 * b2) * scale2

    def other2_of(s, start, sigma):
        b1 = first_other(s, start)
        b2 = other2[s, pl.ds(start, step), :]
        corr = (sigma - theta2 * b2) * inverse_of[s, other_rows(start), :]
        return (corr - weight1 * b1 - weight2 * b2) * scale2

    def cross(s, totals):
        for start in starts:
            here = pl.ds(start, step)
            b3 = last[s, here, :]
            pairs = [(b3, sig1[s, here, :]), (b3, sig2[s, here, :])]
            totals = tuple(t + fold(x * y) for t, (x, y) in zip(totals, pairs))
        return totals

    spread(1, ext3, far3, last, corr2, other2_of, relays[2])
    crossed = lax.fori_loop(0, blocks, cross, (zero,) * 2)
    settle(ext3)

    def sums3(k, totals):
        take(ext3, far3, k, relays[2], 1, far2_of)
        s = turn(k)
        acc[s] = product(ext3, s, True)

        for start in strips:
            here = pl.ds(start, step)
            sigma = acc[s, here, :]
            vectors = [ref[blocks + s, here, :].astype(F32) for ref in (ext1, ext2, ext3)]
            totals = tuple(t + fold(v * sigma) for t, v in zip(totals, vectors))
        return totals

    sum_start(2, list(lax.fori_loop(0, blocks, sums3, (zero,) * 3)) + list(crossed))

    @pl.loop(0, blocks)
    def _(s):
        own = ext3[blocks + s]
        for t in range(terms):
            new = lax.dot_general(
                own, env[t, s], (((0,), (0,)), ((), ())), preferred_element_type=F32
            )
            env[t, s] = (new * width ** (-0.5)).astype(BF16)

    sent(ext3, far3, relays[2], early, 1)
    end = sum_finish(2)
    cells = [
        [theta1, more(10), end(0)],
        [more(11), theta2, end(1)],
        [end(3), end(4), end(2)],
    ]
    row = lax.broadcasted_iota(jnp.int32, (8, 128), 0)
    col = lax.broadcasted_iota(jnp.int32, (8, 128), 1)
    out = zero
    for i in range(3):
        for j in range(3):
            out = jnp.where((row == i) & (col == j), cells[i][j], out)
    proj[...] = out

    for which in range(3):
        arrived(slots.at[which, pl.ds(0, count - 1)], sum_send.at[which])
    for i, (stride, radix) in enumerate(rounds):
        arrived(norm_slots.at[i, pl.ds(0, radix - 1)], norm_send.at[i])


def write_kernel(proj, last, env, proj_out, last_out, env_out, sem):
    copies = [
        pltpu.make_async_copy(last, last_out, sem.at[0]),
        pltpu.make_async_copy(env, env_out, sem.at[1]),
    ]
    for one in copies:
        one.start()
    proj_out[...] = proj[:3, :3]
    for one in copies:
        one.wait()


def write(proj, last, env):
    vmem = pl.BlockSpec(memory_space=pltpu.VMEM)
    anywhere = pl.BlockSpec(memory_space=pl.ANY)
    hbm = pl.BlockSpec(memory_space=pltpu.HBM)
    return pl.pallas_call(
        write_kernel,
        name="write",
        out_shape=(
            jax.ShapeDtypeStruct((3, 3), F32),
            jax.ShapeDtypeStruct(last.shape, F32),
            jax.ShapeDtypeStruct(env.shape, BF16),
        ),
        in_specs=[vmem, anywhere, anywhere],
        out_specs=(vmem, hbm, hbm),
        scratch_shapes=[pltpu.SemaphoreType.DMA((2,))],
        compiler_params=pltpu.CompilerParams(vmem_limit_bytes=12 * 1024 * 1024),
    )(proj, last, env)


HEAD = 3
EARLY = 3
RELAYS = ((0, 4, 4), (0, 0, 0), (3, 6, 6))


def on_device(psi, left, right, connect, sector_dims, precond):
    blocks, width = psi.shape[0], psi.shape[1]
    terms = left.shape[0]
    pieces, devices = lax.axis_size("term"), lax.axis_size("sector")
    count = pieces * devices
    share = width // pieces
    entries = float(blocks * devices * width * width)
    sizes = (pieces, devices, terms, blocks, width, entries)
    others = max(pieces - 1, 1)
    rounds = len(rounds_of(devices))
    early = min(EARLY, blocks) if pieces == 2 else 0
    ahead = max(early, 1)
    dma = pltpu.SemaphoreType.DMA
    vmem = pl.BlockSpec(memory_space=pltpu.VMEM)
    smem = pl.BlockSpec(memory_space=pltpu.SMEM)
    hbm = pl.BlockSpec(memory_space=pltpu.HBM)
    operands = [
        pltpu.with_memory_space_constraint(one, pltpu.HBM)
        for one in (sector_dims, connect, psi, left, right, precond)
    ]
    proj, last, env = pl.pallas_call(
        functools.partial(kernel, sizes, RELAYS, early),
        name="davidson",
        out_shape=(
            jax.ShapeDtypeStruct((8, 128), F32),
            pltpu.VMEM((blocks, share, width), F32),
            pltpu.VMEM((terms, blocks, width, width), BF16),
        ),
        in_specs=[smem, smem, hbm, hbm, hbm, hbm],
        out_specs=(vmem, vmem, vmem),
        scratch_shapes=[
            pltpu.VMEM((terms, blocks, width, width), BF16),
            pltpu.VMEM((terms, blocks, width, width), BF16),
            pltpu.VMEM((blocks, width, width), BF16),
            pltpu.VMEM((blocks, width, width), BF16),
            pltpu.VMEM((blocks, width, width), F32),
            pltpu.VMEM((3 * blocks, width, width), BF16),
            pltpu.VMEM((blocks, width, width), BF16),
            pltpu.VMEM((blocks, width, width), BF16),
            pltpu.VMEM((blocks, width, width), BF16),
            pltpu.VMEM((3 * blocks, width, width), BF16),
            pltpu.VMEM((3 * blocks, width, width), BF16),
            pltpu.VMEM((3 * blocks, width, width), BF16),
            pltpu.VMEM((blocks, width, width), F32),
            pltpu.VMEM((others, blocks, share, width), BF16),
            pltpu.VMEM((others, blocks, share, width), BF16),
            pltpu.VMEM((blocks, share, width), BF16),
            pltpu.VMEM((2, blocks, share, width), BF16),
            pltpu.VMEM((blocks, share, width), F32),
            pltpu.VMEM((blocks, share, width), F32),
            pltpu.VMEM((blocks, share, width), F32),
            pltpu.VMEM((blocks, share, width), F32),
            pltpu.VMEM((blocks, share, width), F32),
            pltpu.VMEM((ahead, width, width), BF16),
            pltpu.VMEM((2, ahead, width, width), BF16),
            pltpu.VMEM((2, ahead, width, width), BF16),
            pltpu.VMEM((ahead, width, width), F32),
            pltpu.VMEM((3, 1, 128), F32),
            pltpu.VMEM((3, count, 1, 128), F32),
            pltpu.VMEM((rounds, 1, 128), F32),
            pltpu.VMEM((rounds, 4, 1, 128), F32),
            dma((pieces, blocks)),
            dma((pieces, blocks)),
            dma((pieces, blocks)),
            dma((pieces, blocks)),
            dma((others, blocks)),
            dma((others, blocks)),
            dma((others, blocks)),
            dma((2, blocks)),
            dma((2, blocks)),
            dma((others, blocks)),
            dma((others, blocks)),
            dma((ahead,)),
            dma((ahead,)),
            dma((2, pieces, ahead)),
            dma((2, pieces, ahead)),
            dma((3,)),
            dma((3,)),
            dma((rounds,)),
            dma((rounds,)),
            dma((4,)),
        ],
        compiler_params=pltpu.CompilerParams(
            collective_id=0, has_side_effects=True, vmem_limit_bytes=48 * 1024 * 1024
        ),
    )(*operands)
    return write(proj, last, env)


def solution(mesh):
    placed = (
        P("sector", None, None),
        P("term", "sector", None, None),
        P("term", "sector", None, None),
        P("term", "sector"),
        P(None, "sector"),
        P("sector", None, None),
    )
    return jax.shard_map(
        on_device,
        mesh=mesh,
        in_specs=placed,
        out_specs=(P(), P("sector", "term", None), P("term", "sector", None, None)),
        check_vma=False,
    )
```

```python
import functools
import jax
import jax.numpy as jnp
from jax import lax
from jax.experimental import pallas as pl
from jax.experimental.pallas import tpu as pltpu
from jax.sharding import PartitionSpec as P

epsilon = 1e-06
MESH = pl.DeviceIdType.MESH
F32 = jnp.float32
BF16 = jnp.bfloat16


def fold(values):
    rows, width = values.shape
    total = values.reshape(rows // 8, 8, width).sum(axis=0)
    out = total[:, :128]
    for start in range(128, width, 128):
        out = out + total[:, start : start + 128]
    return out


def rounds_of(devices):
    out, stride = [], 1
    while stride < devices:
        radix = 4 if devices // stride % 4 == 0 else 2
        out.append((stride, radix))
        stride *= radix
    return out


def kernel(
    sizes, relays, early,
    dims, conn, psi_in, left_in, right_in, pre_in,
    proj, last, env,
    left, right, pre, psi, inverse_of, raw, far1, far2, far3, ext1, ext2, ext3, acc, stage, came, mine, given, other2, sig1, sig2, base1, base2,
    pre_far, sig_out, sig_far, base_far, tile, slots, norm_tile, norm_slots,
    on_send, on_recv, off_send, off_recv, relay_send, share_send, share_recv, mine_send, mine_recv, part_send, part_recv,
    pre_send, pre_recv, sig_send, sig_recv, sum_send, sum_recv, norm_send, norm_recv, load,
):
    pieces, devices, terms, blocks, width, entries = sizes
    share = width // pieces
    count = pieces * devices
    step = min(32, share)
    steps = share // step
    me_t = lax.axis_index("term")
    me_s = lax.axis_index("sector")
    me = me_t * devices + me_s
    first = me_s * blocks - blocks
    paired = pieces == 2
    odd = lax.rem(me_s, 2)
    on_s = me_s + 1 - 2 * odd
    off_s = me_s - 1 + 2 * odd
    has_off = (off_s >= 0) & (off_s < devices)
    zero = jnp.zeros((8, 128), F32)
    rounds = rounds_of(devices)

    def order(k):
        return k + odd * (blocks - 1 - 2 * k)

    def turn(k):
        return blocks - 1 - k + odd * (2 * k - blocks + 1)

    def device_at(offset):
        other = lax.rem(me + offset, count)
        return (other // devices, lax.rem(other, devices))

    def term_at(offset):
        return lax.rem(me_t + offset, pieces)

    def rows_of(piece):
        return pl.ds(pl.multiple_of(piece * share, share), share)

    def part_rows(j):
        return rows_of(term_at(pieces - j))

    everything = pl.ds(0, width)

    def arrived(view, sem):
        pltpu.make_async_copy(view, view, sem).wait()

    loads = [
        pltpu.make_async_copy(source, target, load.at[i])
        for i, (source, target) in enumerate(
            ((psi_in, psi), (pre_in, pre), (left_in, left), (right_in, right))
        )
    ]
    loads[0].start()

    barrier = pltpu.get_barrier_semaphore()

    def greet(t, s):
        pl.semaphore_signal(barrier, inc=1, device_id=(t, s), device_id_type=MESH)

    def peers(stride, radix):
        digit = lax.rem(me_s // stride, radix)
        return digit, [
            me_s + (lax.rem(digit + d, radix) - digit) * stride for d in range(1, radix)
        ]

    greeted = pieces - 1
    for stride, radix in rounds:
        for other in peers(stride, radix)[1]:
            greet(me_t, other)
        greeted += radix - 1
    for j in range(1, pieces):
        greet(term_at(j), me_s)
    apart = has_off & (off_s // rounds[0][1] != me_s // rounds[0][1])

    @pl.when(apart)
    def _():
        greet(me_t, off_s)

    loads[0].wait()
    for one in loads[1:]:
        one.start()


    def on_copy(ref, s, j, rows):
        return pltpu.make_async_remote_copy(
            src_ref=ref.at[blocks + s, rows],
            dst_ref=ref.at[s + odd * 2 * blocks, rows],
            send_sem=on_send.at[j, s],
            recv_sem=on_recv.at[j, s],
            device_id=(me_t, on_s),
            device_id_type=MESH,
        )

    def on_arrived(ref, s, j, rows):
        arrived(ref.at[s + (1 - odd) * 2 * blocks, rows], on_recv.at[j, s])

    def off_copy(ref, far, s, j):
        return pltpu.make_async_remote_copy(
            src_ref=ref.at[blocks + s, part_rows(j)],
            dst_ref=far.at[s, part_rows(j)],
            send_sem=off_send.at[j, s],
            recv_sem=off_recv.at[j, s],
            device_id=(me_t, off_s),
            device_id_type=MESH,
        )

    def off_slot(s):
        return s + odd * 2 * blocks

    def off_arrived(far, s, j):
        arrived(far.at[s, part_rows(j)], off_recv.at[j, s])

    def pre_copy(k):
        return pltpu.make_async_remote_copy(
            src_ref=pre.at[order(k)],
            dst_ref=pre_far.at[k],
            send_sem=pre_send.at[k],
            recv_sem=pre_recv.at[k],
            device_id=(me_t, off_s),
            device_id_type=MESH,
        )

    def sig_copy(which, k, j):
        return pltpu.make_async_remote_copy(
            src_ref=sig_out.at[which, k, part_rows(j)],
            dst_ref=sig_far.at[which, k, part_rows(j)],
            send_sem=sig_send.at[which, j, k],
            recv_sem=sig_recv.at[which, j, k],
            device_id=(me_t, off_s),
            device_id_type=MESH,
        )

    def relay_copy(far, s, j):
        return pltpu.make_async_remote_copy(
            src_ref=far.at[s, rows_of(me_t)],
            dst_ref=far.at[s, rows_of(me_t)],
            send_sem=relay_send.at[j - 1, s],
            recv_sem=off_recv.at[j, s],
            device_id=(term_at(j), me_s),
            device_id_type=MESH,
        )

    def relayed(k, span):
        return (k >= span[0]) & (k < span[1])

    def relay(far, k, span):
        @pl.when(has_off & relayed(k, span))
        def _():
            s = turn(k)
            off_arrived(far, s, 0)
            for j in range(1, pieces):
                relay_copy(far, s, j).start()

    def receive(far, k, span, low):
        s = turn(k)

        @pl.when(has_off & (k >= low) & jnp.logical_not(relayed(k, span)))
        def _():
            off_arrived(far, s, 0)

        @pl.when(has_off & (k >= low))
        def _():
            for j in range(1, pieces):
                off_arrived(far, s, j)

    def sent(ref, far, span, low, which):
        whole = which is None

        @pl.loop(0, blocks)
        def _(k):
            s = order(k)
            if whole:
                on_copy(ref, s, 0, everything).wait_send()
            else:
                for j in range(pieces):
                    on_copy(ref, s, j, part_rows(j)).wait_send()
                if not paired:
                    for offset in range(1, pieces):
                        share_copy(ref, s, offset, me_t).wait_send()

            @pl.when(has_off & (k >= low))
            def _():
                off_copy(ref, far, s, 0).wait_send()

            @pl.when(has_off & (k >= low) & jnp.logical_not(relayed(k, span)))
            def _():
                for j in range(1, pieces):
                    off_copy(ref, far, s, j).wait_send()

            @pl.when(has_off & relayed(k, span))
            def _():
                for j in range(1, pieces):
                    relay_copy(far, turn(k), j).wait_send()

        @pl.when(has_off)
        def _():
            for k in range(early):
                if whole:
                    pre_copy(k).wait_send()
                else:
                    for j in range(pieces):
                        sig_copy(which, k, j).wait_send()

    def share_copy(ref, s, offset, piece):
        return pltpu.make_async_remote_copy(
            src_ref=ref.at[blocks + s, rows_of(piece)],
            dst_ref=ref.at[blocks + s, rows_of(piece)],
            send_sem=share_send.at[offset - 1, s],
            recv_sem=share_recv.at[offset - 1, s],
            device_id=(term_at(offset), me_s),
            device_id_type=MESH,
        )

    def mine_copy(which, s):
        return pltpu.make_async_remote_copy(
            src_ref=mine.at[s],
            dst_ref=given.at[which, s],
            send_sem=mine_send.at[which, s],
            recv_sem=mine_recv.at[which, s],
            device_id=(term_at(1), me_s),
            device_id_type=MESH,
        )

    def part_copy(s, offset):
        return pltpu.make_async_remote_copy(
            src_ref=stage.at[offset - 1, s],
            dst_ref=came.at[offset - 1, s],
            send_sem=part_send.at[offset - 1, s],
            recv_sem=part_recv.at[offset - 1, s],
            device_id=(term_at(offset), me_s),
            device_id_type=MESH,
        )

    lane = lax.broadcasted_iota(jnp.int32, (1, 128), 1)

    def pack(tiles):
        packed = jnp.zeros((1, 128), F32)
        for i, one in enumerate(tiles):
            row = jnp.sum(one, axis=0, keepdims=True)
            packed = jnp.where(lane == i, jnp.sum(row, axis=1, keepdims=True), packed)
        return packed

    def sum_start(which, tiles):
        packed = pack(tiles)
        tile[which] = packed
        slots[which, me] = packed

        @pl.loop(1, count)
        def _(offset):
            pltpu.make_async_remote_copy(
                src_ref=tile.at[which],
                dst_ref=slots.at[which, me],
                send_sem=sum_send.at[which],
                recv_sem=sum_recv.at[which],
                device_id=device_at(offset),
                device_id_type=MESH,
            ).start()

    def sum_finish(which):
        others = slots.at[which, pl.ds(0, count - 1)]
        arrived(others, sum_recv.at[which])
        full = jnp.sum(slots[which], axis=0) / entries
        return lambda i: full[:, i : i + 1]

    def norm_start(i, packed):
        digit, others = peers(*rounds[i])
        norm_tile[i] = packed
        norm_slots[i, digit] = packed
        for other in others:
            pltpu.make_async_remote_copy(
                src_ref=norm_tile.at[i],
                dst_ref=norm_slots.at[i, digit],
                send_sem=norm_send.at[i],
                recv_sem=norm_recv.at[i],
                device_id=(me_t, other),
                device_id_type=MESH,
            ).start()

    def norm_finish(i):
        radix = rounds[i][1]
        arrived(norm_slots.at[i, pl.ds(0, radix - 1)], norm_recv.at[i])
        return jnp.sum(norm_slots[i, pl.ds(0, radix)], axis=0)

    starts = [k * step for k in range(steps)]
    strips = list(range(0, width, step))

    def own_rows(start):
        return pl.ds(pl.multiple_of(me_t * share + start, step), step)

    span0 = relays[0]

    def first_step(k, total):
        s = order(k)
        for start in strips:
            here = pl.ds(start, step)
            rows = lax.broadcasted_iota(jnp.int32, (step, width), 0) + start
            cols = lax.broadcasted_iota(jnp.int32, (step, width), 1)
            keep = (rows < dims[0, s]) & (cols < dims[1, s])
            v = jnp.where(keep, psi[s, here, :].astype(F32), 0.0)
            raw[blocks + s, here, :] = v.astype(BF16)
            total = total + fold(v * v)
        return total

    own_norm = pack([lax.fori_loop(0, blocks, first_step, zero)])
    pl.semaphore_wait(barrier, greeted + apart.astype(jnp.int32))
    norm_start(0, own_norm)

    def first_off(low, high):
        @pl.loop(low, high)
        def _(k):
            s = order(k)

            @pl.when(has_off)
            def _():
                off_copy(raw, far1, s, 0).start()

            @pl.when(has_off & jnp.logical_not(relayed(k, span0)))
            def _():
                for j in range(1, pieces):
                    off_copy(raw, far1, s, j).start()

    first_off(0, HEAD)

    @pl.loop(0, blocks)
    def _(k):
        on_copy(raw, order(k), 0, everything).start()

    def finish_loads():
        loads[1].wait()

        @pl.loop(0, blocks)
        def _(s):
            for start in strips:
                here = pl.ds(start, step)
                inverse_of[s, here, :] = 1.0 / pre[s, here, :].astype(F32)

        @pl.when(has_off)
        def _():
            for k in range(early):
                pre_copy(k).start()

    total = None
    for i in range(len(rounds)):
        total = norm_finish(i)
        if i + 1 < len(rounds):
            norm_start(i + 1, total)
        if i == max(len(rounds) - 2, 0):
            first_off(HEAD, blocks)
            finish_loads()
            for k in range(relays[0][2]):
                relay(far1, k, span0)
    norm = total[:, 0:1] / entries
    scale = 1.0 / jnp.sqrt(norm + epsilon)

    def scaled(source, place, slot):
        for start in strips:
            here = pl.ds(start, step)
            ext1[slot, here, :] = (source[place, here, :].astype(F32) * scale).astype(BF16)

    @pl.loop(0, blocks)
    def _(s):
        scaled(raw, blocks + s, blocks + s)
        for start in starts:
            base1[s, pl.ds(start, step), :] = raw[blocks + s, own_rows(start), :].astype(F32) * scale

    @pl.loop(0, blocks)
    def _(k):
        s = turn(k)
        on_arrived(raw, s, 0, everything)
        slot = s + (1 - odd) * 2 * blocks
        scaled(raw, slot, slot)

    def product(ref, s, keep):
        halves = []
        for t in range(terms):
            source = ref[jnp.clip(conn[t, s] - first, 0, 3 * blocks - 1)]
            one = jnp.dot(left[t, s], source, preferred_element_type=F32).astype(BF16)
            halves.append(one)
            if keep:
                env[t, s] = one
        total = None
        for t in range(terms):
            one = lax.dot_general(
                halves[t], right[t, s], (((1,), (1,)), ((), ())), preferred_element_type=F32
            )
            total = one if total is None else total + one
        return total

    def take(ref, far, k, span, which, far_of):
        s = turn(k)
        low = 0 if which is None else early
        relay(far, k + span[2], span)
        receive(far, k, span, low)

        @pl.when(has_off & (k >= low))
        def _():
            if which is None:
                scaled(far, s, off_slot(s))
            else:
                ref[off_slot(s)] = far[s]

        if low:

            @pl.when(has_off & (k < low))
            def _():
                if which == 0:
                    arrived(pre_far.at[k], pre_recv.at[k])
                for j in range(pieces):
                    arrived(sig_far.at[which, k, part_rows(j)], sig_recv.at[which, j, k])
                for start in strips:
                    here = pl.ds(start, step)
                    b1 = far1[s, here, :].astype(F32) * scale
                    sigma = sig_far[which, k, here, :].astype(F32)
                    inverse = 1.0 / pre_far[k, here, :].astype(F32)
                    ref[off_slot(s), here, :] = far_of(k, here, sigma, b1, inverse).astype(BF16)

    def apply(ref, far, span, which, far_of):
        @pl.loop(0, blocks)
        def _(k):
            take(ref, far, k, span, which, far_of)
            s = turn(k)
            acc[s] = product(ref, s, False)
            for offset in range(1, pieces):
                stage[offset - 1, s] = acc[s, rows_of(term_at(offset)), :].astype(BF16)
                part_copy(s, offset).start()

    def masked(s, base, total):
        rows = lax.broadcasted_iota(jnp.int32, (step, width), 0) + base
        cols = lax.broadcasted_iota(jnp.int32, (step, width), 1)
        return jnp.where((rows < dims[0, s]) & (cols < dims[1, s]), total, 0.0)

    def masked_sum(s, start):
        total = acc[s, own_rows(start), :]
        for offset in range(1, pieces):
            total = total + came[offset - 1, s, pl.ds(start, step), :].astype(F32)
        return masked(s, me_t * share + start, total)

    def other_rows(start):
        return pl.ds(pl.multiple_of(term_at(1) * share + start, step), step)

    def other_sum(which, s, start):
        total = acc[s, other_rows(start), :] + given[which, s, pl.ds(start, step), :].astype(F32)
        return masked(s, term_at(1) * share + start, total)

    def give_blocks(which, low, high):
        if not paired:
            return

        @pl.loop(low, high)
        def _(k):
            s = order(k)
            mine[s] = acc[s, rows_of(me_t), :].astype(BF16)
            mine_copy(which, s).start()

    def give(which):
        if not paired:
            return

        for k in range(early):
            s = order(k)
            for start in starts:
                sigma = (sig1, sig2)[which][s, pl.ds(start, step), :]
                sig_out[which, k, own_rows(start), :] = sigma.astype(BF16)

            @pl.when(has_off)
            def _():
                sig_copy(which, k, 0).start()

        give_blocks(which, FIRST, blocks)

        for k in range(early):
            s = order(k)
            mine_copy(which, s).wait()
            for start in starts:
                sigma = other_sum(which, s, start)
                sig_out[which, k, other_rows(start), :] = sigma.astype(BF16)

            @pl.when(has_off)
            def _():
                sig_copy(which, k, 1).start()

    def divided(s, start):
        return inverse_of[s, own_rows(start), :]

    def part_wait(s):
        for offset in range(1, pieces):
            part_copy(s, offset).wait()

    def spread(which, ref, far, out, corr_of, other_of, span):
        @pl.loop(0, blocks)
        def _(k):
            s = order(k)
            for start in starts:
                value = corr_of(s, start)
                out[s, pl.ds(start, step), :] = value
                ref[blocks + s, own_rows(start), :] = value.astype(BF16)

            if not paired:
                for offset in range(1, pieces):
                    share_copy(ref, s, offset, me_t).start()
            on_copy(ref, s, 0, part_rows(0)).start()

            @pl.when(has_off & (k >= early))
            def _():
                off_copy(ref, far, s, 0).start()

            if paired:
                finish_block(which, ref, far, other_of, span, k)

        if not paired:

            @pl.loop(0, blocks)
            def _(k):
                finish_block(which, ref, far, other_of, span, k)

        for k in range(span[2]):
            relay(far, k, span)

    def finish_block(which, ref, far, other_of, span, k):
        s = order(k)
        if paired:
            @pl.when(k >= early)
            def _():
                mine_copy(which, s).wait()

            for start in starts:
                value = other_of(s, start, other_sum(which, s, start))
                ref[blocks + s, other_rows(start), :] = value.astype(BF16)
        for offset in range(1, pieces):
            if not paired:
                arrived(ref.at[blocks + s, part_rows(offset)], share_recv.at[offset - 1, s])
            on_copy(ref, s, offset, part_rows(offset)).start()

            @pl.when(has_off & (k >= early) & jnp.logical_not(relayed(k, span)))
            def _():
                off_copy(ref, far, s, offset).start()

    def settle(ref):
        @pl.loop(0, blocks)
        def _(k):
            s = turn(k)
            for j in range(pieces):
                on_arrived(ref, s, j, part_rows(j))

    loads[2].wait()
    loads[3].wait()
    apply(ext1, far1, span0, None, None)

    def sums1(k, totals):
        s = turn(k)
        part_wait(s)
        for start in starts:
            totals = sums1_rows(s, start, totals)
        return totals

    def sums1_rows(s, start, totals):
        here = pl.ds(start, step)
        sigma = masked_sum(s, start)
        sig1[s, here, :] = sigma
        inverse = divided(s, start)
        b1 = base1[s, here, :]
        r = sigma * inverse
        q = b1 * inverse
        pairs = [(b1, sigma), (b1, r), (b1, q), (r, r), (r, q), (q, q), (b1, b1)]
        return tuple(t + fold(x * y) for t, (x, y) in zip(totals, pairs))

    give_blocks(0, 0, FIRST)
    sum_start(0, lax.fori_loop(0, blocks, sums1, (zero,) * 7))
    give(0)
    sent(raw, far1, span0, 0, None)
    got = sum_finish(0)
    theta1 = got(0)
    first_gram = got(6)
    weight = got(1) - theta1 * got(2)
    length = (
        (got(3) - 2.0 * theta1 * got(4) + theta1 * theta1 * got(5))
        - 2.0 * weight * weight
        + weight * weight * first_gram
    )
    scale1 = 1.0 / jnp.sqrt(jnp.maximum(length, 0.0) + epsilon)

    def corr1(s, start):
        here = pl.ds(start, step)
        b1 = base1[s, here, :]
        corr = (sig1[s, here, :] - theta1 * b1) * divided(s, start)
        return (corr - weight * b1) * scale1

    def first_other(s, start):
        return raw[blocks + s, other_rows(start), :].astype(F32) * scale

    def other1(s, start, sigma):
        b1 = first_other(s, start)
        corr = (sigma - theta1 * b1) * inverse_of[s, other_rows(start), :]
        value = (corr - weight * b1) * scale1
        other2[s, pl.ds(start, step), :] = value
        return value

    spread(0, ext2, far2, base2, corr1, other1, relays[1])
    settle(ext2)
    def far1_of(k, here, sigma, b1, inverse):
        value = ((sigma - theta1 * b1) * inverse - weight * b1) * scale1
        base_far[k, here, :] = value
        return value

    def far2_of(k, here, sigma, b1, inverse):
        b2 = base_far[k, here, :]
        return ((sigma - theta2 * b2) * inverse - weight1 * b1 - weight2 * b2) * scale2

    apply(ext2, far2, relays[1], 0, far1_of)

    def sums2(k, totals):
        s = turn(k)
        part_wait(s)
        for start in starts:
            totals = sums2_rows(s, start, totals)
        return totals

    def sums2_rows(s, start, totals):
        here = pl.ds(start, step)
        sigma = masked_sum(s, start)
        sig2[s, here, :] = sigma
        inverse = divided(s, start)
        b1 = base1[s, here, :]
        b2 = base2[s, here, :]
        r = sigma * inverse
        q = b2 * inverse
        pairs = [
            (b2, sigma), (b1, r), (b2, r), (b1, q), (b2, q), (r, r), (r, q), (q, q),
            (b1, b2), (b2, b2), (b1, sigma), (b2, sig1[s, here, :]),
        ]
        return tuple(t + fold(x * y) for t, (x, y) in zip(totals, pairs))

    give_blocks(1, 0, FIRST)
    sum_start(1, lax.fori_loop(0, blocks, sums2, (zero,) * 12))
    give(1)
    sent(ext2, far2, relays[1], early, 0)
    more = sum_finish(1)
    theta2 = more(0)
    weight1 = more(1) - theta2 * more(3)
    weight2 = more(2) - theta2 * more(4)
    length2 = (
        (more(5) - 2.0 * theta2 * more(6) + theta2 * theta2 * more(7))
        - 2.0 * (weight1 * weight1 + weight2 * weight2)
        + weight1 * weight1 * first_gram
        + 2.0 * weight1 * weight2 * more(8)
        + weight2 * weight2 * more(9)
    )
    scale2 = 1.0 / jnp.sqrt(jnp.maximum(length2, 0.0) + epsilon)

    def corr2(s, start):
        here = pl.ds(start, step)
        b1 = base1[s, here, :]
        b2 = base2[s, here, :]
        corr = (sig2[s, here, :] - theta2 * b2) * divided(s, start)
        return (corr - weight1 * b1 - weight2 * b2) * scale2

    def other2_of(s, start, sigma):
        b1 = first_other(s, start)
        b2 = other2[s, pl.ds(start, step), :]
        corr = (sigma - theta2 * b2) * inverse_of[s, other_rows(start), :]
        return (corr - weight1 * b1 - weight2 * b2) * scale2

    def cross(s, totals):
        for start in starts:
            here = pl.ds(start, step)
            b3 = last[s, here, :]
            pairs = [(b3, sig1[s, here, :]), (b3, sig2[s, here, :])]
            totals = tuple(t + fold(x * y) for t, (x, y) in zip(totals, pairs))
        return totals

    spread(1, ext3, far3, last, corr2, other2_of, relays[2])
    crossed = lax.fori_loop(0, blocks, cross, (zero,) * 2)
    settle(ext3)

    def sums3(k, totals):
        take(ext3, far3, k, relays[2], 1, far2_of)
        s = turn(k)
        acc[s] = product(ext3, s, True)

        for start in strips:
            here = pl.ds(start, step)
            sigma = acc[s, here, :]
            vectors = [ref[blocks + s, here, :].astype(F32) for ref in (ext1, ext2, ext3)]
            totals = tuple(t + fold(v * sigma) for t, v in zip(totals, vectors))
        return totals

    sum_start(2, list(lax.fori_loop(0, blocks, sums3, (zero,) * 3)) + list(crossed))

    @pl.loop(0, blocks)
    def _(s):
        own = ext3[blocks + s]
        for t in range(terms):
            new = lax.dot_general(
                own, env[t, s], (((0,), (0,)), ((), ())), preferred_element_type=F32
            )
            env[t, s] = (new * width ** (-0.5)).astype(BF16)

    sent(ext3, far3, relays[2], early, 1)
    end = sum_finish(2)
    cells = [
        [theta1, more(10), end(0)],
        [more(11), theta2, end(1)],
        [end(3), end(4), end(2)],
    ]
    row = lax.broadcasted_iota(jnp.int32, (8, 128), 0)
    col = lax.broadcasted_iota(jnp.int32, (8, 128), 1)
    out = zero
    for i in range(3):
        for j in range(3):
            out = jnp.where((row == i) & (col == j), cells[i][j], out)
    proj[...] = out

    for which in range(3):
        arrived(slots.at[which, pl.ds(0, count - 1)], sum_send.at[which])
    for i, (stride, radix) in enumerate(rounds):
        arrived(norm_slots.at[i, pl.ds(0, radix - 1)], norm_send.at[i])


def write_kernel(proj, last, env, proj_out, last_out, env_out, sem):
    copies = [
        pltpu.make_async_copy(last, last_out, sem.at[0]),
        pltpu.make_async_copy(env, env_out, sem.at[1]),
    ]
    for one in copies:
        one.start()
    proj_out[...] = proj[:3, :3]
    for one in copies:
        one.wait()


def write(proj, last, env):
    vmem = pl.BlockSpec(memory_space=pltpu.VMEM)
    anywhere = pl.BlockSpec(memory_space=pl.ANY)
    hbm = pl.BlockSpec(memory_space=pltpu.HBM)
    return pl.pallas_call(
        write_kernel,
        name="write",
        out_shape=(
            jax.ShapeDtypeStruct((3, 3), F32),
            jax.ShapeDtypeStruct(last.shape, F32),
            jax.ShapeDtypeStruct(env.shape, BF16),
        ),
        in_specs=[vmem, anywhere, anywhere],
        out_specs=(vmem, hbm, hbm),
        scratch_shapes=[pltpu.SemaphoreType.DMA((2,))],
        compiler_params=pltpu.CompilerParams(vmem_limit_bytes=12 * 1024 * 1024),
    )(proj, last, env)


HEAD = 3
FIRST = 2
EARLY = 3
RELAYS = ((0, 4, 4), (0, 0, 0), (3, 7, 6))


def on_device(psi, left, right, connect, sector_dims, precond):
    blocks, width = psi.shape[0], psi.shape[1]
    terms = left.shape[0]
    pieces, devices = lax.axis_size("term"), lax.axis_size("sector")
    count = pieces * devices
    share = width // pieces
    entries = float(blocks * devices * width * width)
    sizes = (pieces, devices, terms, blocks, width, entries)
    others = max(pieces - 1, 1)
    rounds = len(rounds_of(devices))
    early = min(EARLY, blocks) if pieces == 2 else 0
    ahead = max(early, 1)
    dma = pltpu.SemaphoreType.DMA
    vmem = pl.BlockSpec(memory_space=pltpu.VMEM)
    smem = pl.BlockSpec(memory_space=pltpu.SMEM)
    hbm = pl.BlockSpec(memory_space=pltpu.HBM)
    operands = [
        pltpu.with_memory_space_constraint(one, pltpu.HBM)
        for one in (sector_dims, connect, psi, left, right, precond)
    ]
    proj, last, env = pl.pallas_call(
        functools.partial(kernel, sizes, RELAYS, early),
        name="davidson",
        out_shape=(
            jax.ShapeDtypeStruct((8, 128), F32),
            pltpu.VMEM((blocks, share, width), F32),
            pltpu.VMEM((terms, blocks, width, width), BF16),
        ),
        in_specs=[smem, smem, hbm, hbm, hbm, hbm],
        out_specs=(vmem, vmem, vmem),
        scratch_shapes=[
            pltpu.VMEM((terms, blocks, width, width), BF16),
            pltpu.VMEM((terms, blocks, width, width), BF16),
            pltpu.VMEM((blocks, width, width), BF16),
            pltpu.VMEM((blocks, width, width), BF16),
            pltpu.VMEM((blocks, width, width), F32),
            pltpu.VMEM((3 * blocks, width, width), BF16),
            pltpu.VMEM((blocks, width, width), BF16),
            pltpu.VMEM((blocks, width, width), BF16),
            pltpu.VMEM((blocks, width, width), BF16),
            pltpu.VMEM((3 * blocks, width, width), BF16),
            pltpu.VMEM((3 * blocks, width, width), BF16),
            pltpu.VMEM((3 * blocks, width, width), BF16),
            pltpu.VMEM((blocks, width, width), F32),
            pltpu.VMEM((others, blocks, share, width), BF16),
            pltpu.VMEM((others, blocks, share, width), BF16),
            pltpu.VMEM((blocks, share, width), BF16),
            pltpu.VMEM((2, blocks, share, width), BF16),
            pltpu.VMEM((blocks, share, width), F32),
            pltpu.VMEM((blocks, share, width), F32),
            pltpu.VMEM((blocks, share, width), F32),
            pltpu.VMEM((blocks, share, width), F32),
            pltpu.VMEM((blocks, share, width), F32),
            pltpu.VMEM((ahead, width, width), BF16),
            pltpu.VMEM((2, ahead, width, width), BF16),
            pltpu.VMEM((2, ahead, width, width), BF16),
            pltpu.VMEM((ahead, width, width), F32),
            pltpu.VMEM((3, 1, 128), F32),
            pltpu.VMEM((3, count, 1, 128), F32),
            pltpu.VMEM((rounds, 1, 128), F32),
            pltpu.VMEM((rounds, 4, 1, 128), F32),
            dma((pieces, blocks)),
            dma((pieces, blocks)),
            dma((pieces, blocks)),
            dma((pieces, blocks)),
            dma((others, blocks)),
            dma((others, blocks)),
            dma((others, blocks)),
            dma((2, blocks)),
            dma((2, blocks)),
            dma((others, blocks)),
            dma((others, blocks)),
            dma((ahead,)),
            dma((ahead,)),
            dma((2, pieces, ahead)),
            dma((2, pieces, ahead)),
            dma((3,)),
            dma((3,)),
            dma((rounds,)),
            dma((rounds,)),
            dma((4,)),
        ],
        compiler_params=pltpu.CompilerParams(
            collective_id=0, has_side_effects=True, vmem_limit_bytes=48 * 1024 * 1024
        ),
    )(*operands)
    return write(proj, last, env)


def solution(mesh):
    placed = (
        P("sector", None, None),
        P("term", "sector", None, None),
        P("term", "sector", None, None),
        P("term", "sector"),
        P(None, "sector"),
        P("sector", None, None),
    )
    return jax.shard_map(
        on_device,
        mesh=mesh,
        in_specs=placed,
        out_specs=(P(), P("sector", "term", None), P("term", "sector", None, None)),
        check_vma=False,
    )
```
